256 devices in a mesh: replica: 16 (over z_hi, y), tensor: 16 (over x, z_lo, core).
Axes of the slice: x: 4, y: 4, z: 8 (z_hi: 4, z_lo: 2; z = z_hi * 2 + z_lo), core: 2. Of those that a mesh axis runs over, the one named last changes fastest.
Arguments:
- activations: bfloat16 [16384, 2048], P('replica', 'tensor'), may hold values from -0.625 to 0.625
- grad_out: bfloat16 [16384, 7168], P('replica', 'tensor'), may hold values from -6 to 6
- weight: bfloat16 [2048, 7168], P(None, 'tensor'), may hold values from -0.0625 to 0.0625
- momentum: float32 [16, 2048, 7168], P('replica', None, 'tensor'), may hold values from -6 to 6
- freq_rows: int32 [16, 32, 112], P(None, None, 'tensor'), may hold values from 0 to 63
Outputs:
- input_grad: bfloat16 [16384, 2048], P('replica', 'tensor')
- momentum_out: float32 [16, 2048, 7168], P('replica', None, 'tensor')
- update: bfloat16 [2048, 7168], P(None, 'tensor')
The draws below stay inside these ranges and needn't reach their ends.
All inputs are finite; a program needn't handle non-finite values.
Results may differ from the reference program's by a relative error of at most 0.001.
Values may be sent and summed in bfloat16 or wider, within the bound.
A program may use at most 128 MiB of HBM per device.

```python
import jax
import jax.numpy as jnp
from jax import lax

D = 2048
FF = 7168
TILE = 64
TOK_DEV = 1024
TOKENS = 16384
TILE_ROWS = 32
TILE_COLS = 112
N_REPLICA = 16


def touch_ends(entries, stream_key, smallest, largest):
    longest = entries.shape.index(max(entries.shape))
    spots = []
    for shift in (0, 1):
        where = [jax.random.randint(jax.random.fold_in(stream_key, axis), (), 0, length) for axis, length in enumerate(entries.shape)]
        where[longest] = (where[longest] + shift) % entries.shape[longest]
        spots.append(tuple(where))
    return entries.at[spots[0]].set(smallest).at[spots[1]].set(largest)


def level_of(rng, extent, cuts, smallest, largest):
    loudness = 1.0
    for axis_at, blocks in cuts:
        steps = jax.random.uniform(jax.random.fold_in(jax.random.fold_in(rng, 6), axis_at), (blocks,), jnp.float32, smallest / len(cuts), largest / len(cuts))
        loudness = loudness * jnp.repeat(jnp.exp(steps), extent[axis_at] // blocks).reshape((-1,) + (1,) * (len(extent) - 1 - axis_at))
    return loudness


def scatter_about(key, shape, deviation, reach, cuts=(), kind=jnp.bfloat16):
    values = deviation * jax.random.normal(key, shape, jnp.float32)
    if cuts:
        values = values * level_of(key, shape, cuts, -0.22, 0.18)
    return jnp.clip(values, -reach, reach).astype(kind)


def setup_inputs(seed: int = 0) -> dict:
    splits = jax.random.split(jax.random.key(seed), 6)
    return {
        "activations": scatter_about(splits[0], (TOKENS, D), 0.04, 0.625, ((0, 16), (1, 16))),
        "grad_out": scatter_about(splits[1], (TOKENS, FF), 1.0, 6.0, ((0, 16), (1, 16))),
        "weight": scatter_about(splits[2], (D, FF), FF ** -0.5, 0.0625, ((1, 16),)),
        "momentum": scatter_about(splits[3], (N_REPLICA, D, FF), 1.0, 6.0, ((0, 16), (2, 16)), jnp.float32),
        "freq_rows": touch_ends(jax.random.randint(splits[4], (N_REPLICA, TILE_ROWS, TILE_COLS), 0, TILE), jax.random.fold_in(splits[4], 1), 0, TILE - 1).astype(jnp.int32),
    }


decay_rate = 0.9
highest = lax.Precision.HIGHEST

def cosine_table():
    freq = jnp.arange(TILE, dtype=jnp.float32)[:, None]
    place = jnp.arange(TILE, dtype=jnp.float32)[None, :]
    values = jnp.cos(jnp.pi * (2.0 * place + 1.0) * freq / (2.0 * TILE)) * jnp.sqrt(2.0 / TILE)
    return jnp.where(freq == 0.0, values / jnp.sqrt(2.0), values)

def one_replica(inputs):
    acts, grads, moment, chosen = inputs
    basis = cosine_table()
    weight_grad = jnp.dot(acts.T, grads, preferred_element_type=jnp.float32)
    kept = decay_rate * moment + weight_grad
    tile_view = kept.reshape(TILE_ROWS, TILE, TILE_COLS, TILE)
    half_done = jnp.einsum('ancm,lm->ancl', tile_view, basis, precision=highest)
    onehot = (chosen[:, :, None] == jnp.arange(TILE, dtype=jnp.int32)[None, None, :]).astype(jnp.float32)
    picked = jnp.einsum('ack,kn->acn', onehot, basis, precision=highest)
    coeff_rows = jnp.einsum('acn,ancl->acl', picked, half_done, precision=highest)
    spread = jnp.einsum('acj,jm->acm', coeff_rows, basis, precision=highest)
    removed = jnp.einsum('acn,acm->ancm', picked, spread)
    return (kept - removed.reshape(D, FF), coeff_rows)

def reference(activations, grad_out, weight, momentum, freq_rows):
    basis = cosine_table()
    input_grad = lax.dot_general(grad_out, weight, (((1,), (1,)), ((), ())), preferred_element_type=jnp.float32).astype(jnp.bfloat16)
    acts = activations.reshape(N_REPLICA, TOK_DEV, D)
    grads = grad_out.reshape(N_REPLICA, TOK_DEV, FF)
    momentum_out, coeff_all = lax.map(one_replica, (acts, grads, momentum, freq_rows))
    onehot = (freq_rows[..., None] == jnp.arange(TILE, dtype=jnp.int32)).astype(jnp.float32)
    summed = jnp.einsum('rack,racj->ackj', onehot, coeff_all, precision=highest)
    right_done = jnp.einsum('ackj,jm->ackm', summed, basis, precision=highest)
    decoded = jnp.einsum('kn,ackm->ancm', basis, right_done, precision=highest)
    update = decoded.reshape(D, FF).astype(jnp.bfloat16)
    return (input_grad, momentum_out, update)
```

```python
import functools

import jax
import jax.numpy as jnp
import numpy as np
from jax import lax
from jax.experimental import pallas as pl
from jax.experimental.pallas import tpu as pltpu
from jax.sharding import PartitionSpec as P

MESH = pl.DeviceIdType.MESH
F32 = jnp.float32
BF16 = jnp.bfloat16

TILE = 64
decay_rate = 0.9


def cosine_pieces():
    freq = np.arange(TILE, dtype=np.float64)[:, None]
    place = np.arange(TILE, dtype=np.float64)[None, :]
    values = np.cos(np.pi * (2.0 * place + 1.0) * freq / (2.0 * TILE)) * np.sqrt(2.0 / TILE)
    values = np.where(freq == 0.0, values / np.sqrt(2.0), values).T
    rest = values.astype(np.float32)
    terms = []
    for _ in range(3):
        term = rest.astype(BF16)
        terms.append(term)
        rest = rest - term.astype(np.float32)
    terms.append(np.zeros_like(terms[0]))
    return np.concatenate(terms, axis=1)


def kernel(
    act_hbm, go_hbm, w_hbm, mom_hbm, freq_ref, cos_ref,
    ig_hbm, mo_hbm, up_hbm,
    act_raw, acts, go, wt, q, rx, zr, mom, gtmp, basis, left_side, p_own, p_all, upd, ig, fexp, vexp,
    load_sem, store_sem, ex_send, ex_recv, ag_send, ag_recv, sib_send, sib_recv,
    rs_send, rs_recv, zs_send, zs_recv, ps_send, ps_recv, py_send, py_recv,
):
    r = lax.axis_index("replica")
    t = lax.axis_index("tensor")
    x, z, c = t // 4, (t // 2) % 2, t % 2
    zh, y = r // 4, r % 4
    other = 1 - z

    def at(x_, z_, c_):
        return (r, x_ * 4 + z_ * 2 + c_)

    xr, xl, xo = (x + 1) % 4, (x + 3) % 4, (x + 2) % 4
    right, left = at(xr, z, c), at(xl, z, c)
    zdev, sib = at(x, other, c), at(x, z, 1 - c)
    zh_devs = [(((zh + k) % 4) * 4 + y, t) for k in (1, 2, 3)]
    y_devs = [(zh * 4 + (y + k) % 4, t) for k in (1, 2, 3)]

    loads = [
        pltpu.make_async_copy(act_hbm, act_raw, load_sem.at[0]),
        pltpu.make_async_copy(go_hbm, go.at[0], load_sem.at[1]),
        pltpu.make_async_copy(w_hbm.at[:, c], wt.at[0], load_sem.at[2]),
        pltpu.make_async_copy(mom_hbm, mom, load_sem.at[3]),
    ]
    for load in loads:
        load.start()

    barrier = pltpu.get_barrier_semaphore()
    peers = [right, left, zdev, sib] + zh_devs + y_devs
    for peer in peers:
        pl.semaphore_signal(barrier, inc=1, device_id=peer, device_id_type=MESH)

    loads[0].wait()
    acts[t] = jnp.transpose(act_raw[...])
    pl.semaphore_wait(barrier, len(peers))

    def remote(src, dst, send, recv, dev):
        return pltpu.make_async_remote_copy(
            src_ref=src, dst_ref=dst, send_sem=send, recv_sem=recv, device_id=dev, device_id_type=MESH
        )

    sent = []

    def push(src, dst, send, recv, dev):
        copy = remote(src, dst, send, recv, dev)
        copy.start()
        sent.append(copy)

    def block(x_, z_, c_):
        return acts.at[x_ * 4 + z_ * 2 + c_]

    def half(x_, z_, c_, k):
        return acts.at[x_ * 4 + z_ * 2 + c_, pl.ds(k * 64, 64)]

    def push_same(ref, sends, recvs, k, dev):
        push(ref, ref, sends.at[k], recvs.at[k], dev)

    def arrived(ref, sends, recvs, k):
        remote(ref, ref, sends.at[k], recvs.at[k], sib).wait_recv()

    own = block(x, z, c)
    push_same(own, ag_send, ag_recv, 0, right)
    push_same(own, ag_send, ag_recv, 1, left)
    push_same(own, ag_send, ag_recv, 4, zdev)
    push(go_hbm, go.at[1], ex_send.at[0], ex_recv.at[0], sib)
    push(w_hbm.at[:, 1 - c], wt.at[1], ex_send.at[1], ex_recv.at[1], sib)
    push_same(own, sib_send, sib_recv, 0, sib)

    lane_tile = lax.broadcasted_iota(jnp.int32, (32, 448), 1) // TILE
    mine = freq_ref[r]
    spread = jnp.zeros((32, 448), jnp.int32)
    for k in range(7):
        spread = jnp.where(lane_tile == k, mine[:, k : k + 1], spread)
    fexp[...] = spread
    lane = lax.broadcasted_iota(jnp.int32, (32, 128), 1)
    folded = jnp.full((32, 128), -1, jnp.int32)
    for rep in range(16):
        rows = freq_ref[rep]
        for k in range(7):
            folded = jnp.where(lane == k * 16 + rep, rows[:, k : k + 1], folded)
    vexp[...] = folded

    def onehot4(row, width):
        hot = (lax.broadcasted_iota(jnp.int32, (TILE, width), 0) == row).astype(F32).astype(BF16)
        return jnp.concatenate([hot] * 4, axis=0)

    @pl.loop(0, 32)
    def _(a):
        rows = pl.ds(pl.multiple_of(a * TILE, TILE), TILE)
        basis[rows, :] = jnp.dot(cos_ref[...], onehot4(fexp[pl.ds(a, 1), :], 448), preferred_element_type=F32)
        side = jnp.dot(cos_ref[...], onehot4(vexp[pl.ds(a, 1), :], 128), preferred_element_type=F32)
        high = side.astype(BF16)
        low = (side - high.astype(F32)).astype(BF16)
        left_side[rows, :] = jnp.concatenate([high, high, low], axis=1)

    loads[1].wait()
    loads[2].wait()
    remote(go.at[0], go.at[1], ex_send.at[0], ex_recv.at[0], sib).wait_recv()
    remote(wt.at[0], wt.at[1], ex_send.at[1], ex_recv.at[1], sib).wait_recv()

    def share(dx):
        dest = (x + dx) % 4

        @pl.loop(0, 4)
        def _(k):
            rows = pl.ds(pl.multiple_of(k * 256, 256), 256)
            total = jnp.zeros((256, 256), F32)
            for part in range(2):
                wpair = wt[part, pl.ds(dest * 2, 2)].reshape(256, 448)
                total += lax.dot_general(
                    go[part, rows, :], wpair, (((1,), (1,)), ((), ())), preferred_element_type=F32
                )
            q[dx, 0, rows, :] = total[:, :128]
            q[dx, 1, rows, :] = total[:, 128:]

    top, bottom = pl.ds(0, 512), pl.ds(512, 512)
    zs = (other, z)

    def rs_push(src, direction, kind, zi):
        k = (direction * 3 + kind) * 2 + zi
        push(src, rx.at[direction, kind, zi], rs_send.at[k], rs_recv.at[k], (right, left)[direction])

    def rs_wait(direction, kind, zi):
        k = (direction * 3 + kind) * 2 + zi
        slot = rx.at[direction, kind, zi]
        remote(slot, slot, rs_send.at[k], rs_recv.at[k], sib).wait_recv()

    share(2)
    rs_push(q.at[2, zs[0], top], 0, 0, 0)
    rs_push(q.at[2, zs[0], bottom], 1, 0, 0)
    share(1)
    rs_push(q.at[1, zs[0], bottom], 0, 1, 0)
    share(3)
    rs_push(q.at[3, zs[0], top], 1, 1, 0)
    share(0)

    def from_x(x_, k, fwd_half, fwd_k, fwd_dev, zk):
        blk = block(x_, z, c)
        arrived(blk, ag_send, ag_recv, k)
        push_same(half(x_, z, c, fwd_half), ag_send, ag_recv, fwd_k, fwd_dev)
        push_same(blk, ag_send, ag_recv, zk, zdev)
        push_same(blk, sib_send, sib_recv, zk - 4, sib)

    from_x(xl, 0, 0, 2, right, 5)
    from_x(xr, 1, 1, 3, left, 6)
    rs_push(q.at[2, zs[1], top], 0, 0, 1)
    rs_push(q.at[2, zs[1], bottom], 1, 0, 1)
    rs_push(q.at[1, zs[1], bottom], 0, 1, 1)
    rs_push(q.at[3, zs[1], top], 1, 1, 1)

    loads[3].wait()

    def unit(x_, z_):
        u = x_ * 2 + z_
        pair = acts[pl.ds(u * 2, 2)].reshape(256, 1024)
        gtmp[...] = jnp.dot(pair, go[0], preferred_element_type=F32)
        base = u * 256

        @pl.loop(0, 4)
        def _(s):
            rows = pl.ds(pl.multiple_of(base + s * TILE, TILE), TILE)
            kept = decay_rate * mom[rows, :] + gtmp[pl.ds(pl.multiple_of(s * TILE, TILE), TILE), :]
            mine = basis[rows, :]
            line = jnp.sum(mine * kept, axis=0, keepdims=True)
            mom[rows, :] = kept - mine * line
            p_own[z_, pl.ds(x_ * 4 + s, 1), :] = line

        rows = pl.ds(pl.multiple_of(base, 256), 256)
        copy = pltpu.make_async_copy(mom.at[rows], mo_hbm.at[rows], store_sem.at[len(stores)])
        copy.start()
        stores.append(copy)

    stores = []
    sb = lambda x_, z_: block(x_, z_, 1 - c)
    sh = lambda x_, z_, k: half(x_, z_, 1 - c, k)

    arrived(sb(x, z), sib_send, sib_recv, 0)
    unit(x, z)
    arrived(sb(xl, z), sib_send, sib_recv, 1)
    unit(xl, z)
    arrived(sb(xr, z), sib_send, sib_recv, 2)
    unit(xr, z)
    for k in range(2):
        piece = half(xo, z, c, k)
        arrived(piece, ag_send, ag_recv, 2 + k)
        push_same(piece, ag_send, ag_recv, 7 + k, zdev)
        push_same(piece, sib_send, sib_recv, 3 + k, sib)
    for k in range(2):
        arrived(sh(xo, z, k), sib_send, sib_recv, 3 + k)
    unit(xo, z)

    def p_zh(group, z_):
        rows = pl.ds(pl.multiple_of(z_ * 16, 16), 16)
        p_all[zh, y, rows, :] = p_own[z_]
        mine = p_all.at[zh, y, rows]
        for k, dev in enumerate(zh_devs):
            push(mine, mine, ps_send.at[group, k], ps_recv.at[group, k], dev)

    def p_y(group, z_):
        rows = pl.ds(pl.multiple_of(z_ * 16, 16), 16)
        for k in range(3):
            slot = p_all.at[(zh + 3 - k) % 4, y, rows]
            remote(slot, slot, ps_send.at[group, k], ps_recv.at[group, k], sib).wait_recv()
        mine = p_all.at[:, y, rows]
        for k, dev in enumerate(y_devs):
            push(mine, mine, py_send.at[group, k], py_recv.at[group, k], dev)

    def p_done(group, z_):
        rows = pl.ds(pl.multiple_of(z_ * 16, 16), 16)
        for k in range(3):
            slot = p_all.at[:, (y + 3 - k) % 4, rows]
            remote(slot, slot, py_send.at[group, k], py_recv.at[group, k], sib).wait_recv()

    tiles = lax.broadcasted_iota(jnp.int32, (16, 448), 1) // TILE

    def decode(z_):
        @pl.loop(0, 16)
        def _(i):
            a = (i // 4) * 8 + z_ * 4 + i % 4
            row = pl.ds(z_ * 16 + i, 1)
            p16 = jnp.concatenate([p_all[k // 4, k % 4, row, :] for k in range(16)], axis=0)
            high = p16.astype(BF16).astype(F32)
            low = p16 - high
            zero = jnp.zeros_like(p16)
            highs = [jnp.where(tiles == k, high, zero).astype(BF16) for k in range(7)] + [zero.astype(BF16)]
            lows = [jnp.where(tiles == k, low, zero).astype(BF16) for k in range(7)] + [zero.astype(BF16)]
            full = jnp.concatenate(highs + lows + highs, axis=0)
            rows = pl.ds(pl.multiple_of(a * TILE, TILE), TILE)
            upd[rows, :] = jnp.dot(left_side[rows, :], full, preferred_element_type=F32).astype(BF16)

        for k in range(4):
            rows = pl.ds(pl.multiple_of((k * 2 + z_) * 256, 256), 256)
            copy = pltpu.make_async_copy(upd.at[rows], up_hbm.at[rows], store_sem.at[len(stores)])
            copy.start()
            stores.append(copy)

    p_zh(0, z)

    def rs_second(zi):
        rs_wait(0, 0, zi)
        q[1, zs[zi], top, :] += rx[0, 0, zi]
        rs_push(q.at[1, zs[zi], top], 0, 2, zi)
        rs_wait(1, 0, zi)
        q[3, zs[zi], bottom, :] += rx[1, 0, zi]
        rs_push(q.at[3, zs[zi], bottom], 1, 2, zi)

    rs_second(0)
    p_y(0, z)

    def from_z(x_, zk):
        blk = block(x_, other, c)
        arrived(blk, ag_send, ag_recv, zk)
        push_same(blk, sib_send, sib_recv, zk + 1, sib)

    from_z(x, 4)
    from_z(xl, 5)
    from_z(xr, 6)
    arrived(sb(x, other), sib_send, sib_recv, 5)
    unit(x, other)
    arrived(sb(xl, other), sib_send, sib_recv, 6)
    unit(xl, other)
    arrived(sb(xr, other), sib_send, sib_recv, 7)
    unit(xr, other)
    rs_second(1)
    for k in range(2):
        piece = half(xo, other, c, k)
        arrived(piece, ag_send, ag_recv, 7 + k)
        push_same(piece, sib_send, sib_recv, 8 + k, sib)
    for k in range(2):
        arrived(sh(xo, other, k), sib_send, sib_recv, 8 + k)
    unit(xo, other)
    p_zh(1, other)

    def x_sum(zi):
        for direction in range(2):
            for kind in (1, 2):
                rs_wait(direction, kind, zi)
        q[0, zs[zi], top, :] += rx[0, 2, zi] + rx[1, 1, zi]
        q[0, zs[zi], bottom, :] += rx[0, 1, zi] + rx[1, 2, zi]

    x_sum(0)
    push(q.at[0, other], zr, zs_send, zs_recv, zdev)
    p_done(0, z)
    decode(z)
    p_y(1, other)
    p_done(1, other)
    decode(other)

    x_sum(1)
    remote(q.at[0, other], zr, zs_send, zs_recv, zdev).wait_recv()
    ig[...] = (q[0, z] + zr[...]).astype(BF16)
    last = pltpu.make_async_copy(ig, ig_hbm, store_sem.at[len(stores)])
    last.start()
    for copy in stores:
        copy.wait()
    last.wait()
    for copy in sent:
        copy.wait_send()


def body(activations, grad_out, weight, momentum, freq_rows):
    hbm = pl.BlockSpec(memory_space=pl.ANY)
    vmem = pl.BlockSpec(memory_space=pltpu.VMEM)
    dma = pltpu.SemaphoreType.DMA
    input_grad, momentum_out, update = pl.pallas_call(
        kernel,
        out_shape=(
            jax.ShapeDtypeStruct((1024, 128), BF16),
            jax.ShapeDtypeStruct((2048, 448), F32),
            jax.ShapeDtypeStruct((2048, 448), BF16),
        ),
        in_specs=[hbm, hbm, hbm, hbm, vmem, vmem],
        out_specs=(hbm, hbm, hbm),
        scratch_shapes=[
            pltpu.VMEM((1024, 128), BF16),
            pltpu.VMEM((16, 128, 1024), BF16),
            pltpu.VMEM((2, 1024, 448), BF16),
            pltpu.VMEM((2, 8, 128, 448), BF16),
            pltpu.VMEM((4, 2, 1024, 128), F32),
            pltpu.VMEM((2, 3, 2, 512, 128), F32),
            pltpu.VMEM((1024, 128), F32),
            pltpu.VMEM((2048, 448), F32),
            pltpu.VMEM((256, 448), F32),
            pltpu.VMEM((2048, 448), F32),
            pltpu.VMEM((2048, 384), BF16),
            pltpu.VMEM((2, 16, 448), F32),
            pltpu.VMEM((4, 4, 32, 448), F32),
            pltpu.VMEM((2048, 448), BF16),
            pltpu.VMEM((1024, 128), BF16),
            pltpu.VMEM((32, 448), jnp.int32),
            pltpu.VMEM((32, 128), jnp.int32),
            dma((4,)), dma((17,)),
            dma((2,)), dma((2,)),
            dma((9,)), dma((9,)),
            dma((10,)), dma((10,)),
            dma((12,)), dma((12,)),
            dma, dma,
            dma((2, 3)), dma((2, 3)),
            dma((2, 3)), dma((2, 3)),
        ],
        compiler_params=pltpu.CompilerParams(
            collective_id=0, has_side_effects=True, vmem_limit_bytes=52 * 1024 * 1024
        ),
        name="demo_step",
    )(
        activations,
        grad_out,
        weight.reshape(8, 2, 128, 448),
        momentum[0],
        freq_rows,
        jnp.asarray(cosine_pieces()),
    )
    return input_grad, momentum_out[None], update


def solution(mesh):
    placed = (
        P("replica", "tensor"),
        P("replica", "tensor"),
        P(None, "tensor"),
        P("replica", None, "tensor"),
        P(None, None, "tensor"),
    )
    return jax.shard_map(
        body,
        mesh=mesh,
        in_specs=placed,
        out_specs=(P("replica", "tensor"), P("replica", None, "tensor"), P(None, "tensor")),
        check_vma=False,
    )
```

```python
import functools

import jax
import jax.numpy as jnp
import numpy as np
from jax import lax
from jax.experimental import pallas as pl
from jax.experimental.pallas import tpu as pltpu
from jax.sharding import PartitionSpec as P

MESH = pl.DeviceIdType.MESH
F32 = jnp.float32
BF16 = jnp.bfloat16

TILE = 64
decay_rate = 0.9


def cosine_tables():
    freq = np.arange(TILE, dtype=np.float64)[:, None]
    place = np.arange(TILE, dtype=np.float64)[None, :]
    values = np.cos(np.pi * (2.0 * place + 1.0) * freq / (2.0 * TILE)) * np.sqrt(2.0 / TILE)
    values = np.where(freq == 0.0, values / np.sqrt(2.0), values).astype(np.float32)
    high = values.astype(BF16)
    low = (values - high.astype(np.float32)).astype(BF16)
    return np.concatenate([values] * 2, axis=1), np.concatenate([high] * 4 + [low] * 4, axis=1)


def kernel(
    act_hbm, go_hbm, w_hbm, mom_hbm, freq_hbm, cos_hbm, terms_hbm,
    ig_hbm, mo_hbm, up_hbm,
    acts, got, go, wt, q, sx, rx, sz, rz, mom, gtmp, ptmp, ycat, basis, segments, right_side, lhs, p_own, p_all, upd, ig,
    freq_ref, cos_ref, terms_ref,
    load_sem, store_sem, ex_send, ex_recv, ag_send, ag_recv, sib_send, sib_recv,
    rs_send, rs_recv, zs_send, zs_recv, ps_send, ps_recv, py_send, py_recv,
):
    r = lax.axis_index("replica")
    t = lax.axis_index("tensor")
    x, z, c = t // 4, (t // 2) % 2, t % 2
    zh, y = r // 4, r % 4
    other = 1 - z

    def at(x_, z_, c_):
        return (r, x_ * 4 + z_ * 2 + c_)

    xr, xl, xo = (x + 1) % 4, (x + 3) % 4, (x + 2) % 4
    right, left = at(xr, z, c), at(xl, z, c)
    zdev, sib = at(x, other, c), at(x, z, 1 - c)
    zh_devs = [(((zh + k) % 4) * 4 + y, t) for k in (1, 2, 3)]
    y_devs = [(zh * 4 + (y + k) % 4, t) for k in (1, 2, 3)]

    def w_cols(u, c_):
        return w_hbm.at[:, pl.ds(pl.multiple_of((2 * u + c_) * 128, 128), 128)]

    loads = [
        pltpu.make_async_copy(go_hbm, got, load_sem.at[0]),
        pltpu.make_async_copy(act_hbm, acts.at[t], load_sem.at[1]),
        pltpu.make_async_copy(freq_hbm, freq_ref, load_sem.at[2]),
        pltpu.make_async_copy(cos_hbm, cos_ref, load_sem.at[3]),
        pltpu.make_async_copy(terms_hbm, terms_ref, load_sem.at[4]),
    ] + [pltpu.make_async_copy(w_cols(u, c), wt.at[0, u], load_sem.at[5 + u]) for u in range(8)]
    loads.append(pltpu.make_async_copy(mom_hbm, mom, load_sem.at[13]))
    for load in loads:
        load.start()

    barrier = pltpu.get_barrier_semaphore()
    peers = [right, left, zdev, sib] + zh_devs + y_devs
    for peer in peers:
        pl.semaphore_signal(barrier, inc=1, device_id=peer, device_id_type=MESH)

    loads[0].wait()
    go[0] = jnp.transpose(got[...])
    loads[1].wait()
    pl.semaphore_wait(barrier, len(peers))

    def remote(src, dst, send, recv, dev):
        return pltpu.make_async_remote_copy(
            src_ref=src, dst_ref=dst, send_sem=send, recv_sem=recv, device_id=dev, device_id_type=MESH
        )

    sent = []

    def push(src, dst, send, recv, dev):
        copy = remote(src, dst, send, recv, dev)
        copy.start()
        sent.append(copy)

    def block(x_, z_, c_):
        return acts.at[x_ * 4 + z_ * 2 + c_]

    def half(x_, z_, c_, h):
        return acts.at[x_ * 4 + z_ * 2 + c_, h]

    def pair(x_, z_, c_, k):
        return acts.at[x_ * 4 + z_ * 2 + c_, :, k]

    def quarter(x_, z_, c_, h, k):
        return acts.at[x_ * 4 + z_ * 2 + c_, h, k]

    def push_same(ref, sends, recvs, k, dev):
        push(ref, ref, sends.at[k], recvs.at[k], dev)

    def arrived(ref, sends, recvs, k):
        remote(ref, ref, sends.at[k], recvs.at[k], sib).wait_recv()

    own = block(x, z, c)
    push_same(own, ag_send, ag_recv, 0, right)
    push_same(own, ag_send, ag_recv, 1, left)
    push_same(own, ag_send, ag_recv, 2, zdev)
    push(go.at[0], go.at[1], ex_send.at[0], ex_recv.at[0], sib)
    for u in range(8):
        push(w_cols(u, 1 - c), wt.at[1, u], ex_send.at[1 + u], ex_recv.at[1 + u], sib)
    push_same(own, sib_send, sib_recv, 0, sib)

    for load in loads[2:5]:
        load.wait()

    mine = jnp.concatenate([freq_ref[k, pl.ds(r, 1), :] for k in range(7)], axis=0)
    first = lax.broadcasted_iota(jnp.int32, (7, 128), 1) < TILE
    spread = jnp.concatenate(
        [jnp.where(first, mine[:, 2 * k : 2 * k + 1], mine[:, 2 * k + 1 : 2 * k + 2]) for k in range(16)], axis=1
    )

    def pick(k, so_far):
        row = jnp.concatenate([cos_ref[pl.ds(k, 1), :]] * 16, axis=1)
        return jnp.where(spread == k, row, so_far)

    basis[...] = lax.fori_loop(0, TILE, pick, jnp.zeros((7, 2048), F32))

    segments[...] = (
        lax.broadcasted_iota(jnp.int32, (512, 256), 0) % 256 // TILE
        == lax.broadcasted_iota(jnp.int32, (512, 256), 1) // TILE
    ).astype(F32).astype(BF16)
    chooser = (
        lax.broadcasted_iota(jnp.int32, (8, 512), 1) % 256 // TILE
        == lax.broadcasted_iota(jnp.int32, (8, 512), 0)
    ).astype(F32).astype(BF16)

    widen = (
        lax.broadcasted_iota(jnp.int32, (TILE, 16), 0) // 4 == lax.broadcasted_iota(jnp.int32, (TILE, 16), 1)
    ).astype(F32).astype(BF16)
    wide = jnp.concatenate(
        [jnp.dot(widen, freq_ref[k].astype(F32).astype(BF16), preferred_element_type=F32) for k in range(7)], axis=0
    )
    keep = (
        lax.broadcasted_iota(jnp.int32, (448, 32), 0) % 4 == lax.broadcasted_iota(jnp.int32, (448, 32), 1) % 4
    )
    narrow = (
        lax.broadcasted_iota(jnp.int32, (32, 8), 0) // 4 == lax.broadcasted_iota(jnp.int32, (32, 8), 1)
    ).astype(F32).astype(BF16)
    columns = jnp.dot(jnp.where(keep, wide, 0.0).astype(BF16), narrow, preferred_element_type=F32)
    freq_lane = lax.broadcasted_iota(jnp.int32, (448, TILE), 1).astype(F32)
    same = (
        lax.broadcasted_iota(jnp.int32, (TILE, 256), 0) % 4 == lax.broadcasted_iota(jnp.int32, (TILE, 256), 1) // TILE
    )
    for u in range(8):
        hot = (columns[:, u : u + 1] == freq_lane).astype(F32).astype(BF16)
        both = jnp.dot(hot, terms_ref[...], preferred_element_type=F32)
        for k in range(7):
            rows = both[k * TILE : (k + 1) * TILE]
            right_side[u, k, pl.ds(0, TILE), :] = jnp.where(same, rows[:, :256], 0.0).astype(BF16)
            right_side[u, k, pl.ds(TILE, TILE), :] = jnp.where(same, rows[:, 256:], 0.0).astype(BF16)

    for load in loads[5:13]:
        load.wait()
    remote(go.at[0], go.at[1], ex_send.at[0], ex_recv.at[0], sib).wait_recv()
    for u in range(8):
        remote(wt.at[0, u], wt.at[1, u], ex_send.at[1 + u], ex_recv.at[1 + u], sib).wait_recv()

    def share(dx):
        dest = (x + dx) % 4

        @pl.loop(0, 4)
        def _(k):
            rows = pl.ds(pl.multiple_of(k * 256, 256), 256)
            total = jnp.zeros((256, 256), F32)
            for part in range(2):
                pair = jnp.concatenate([wt[part, dest * 2], wt[part, dest * 2 + 1]], axis=1)
                total += jnp.dot(go[part, rows, :], pair, preferred_element_type=F32)
            q[dx, 0, rows, :] = total[:, :128]
            q[dx, 1, rows, :] = total[:, 128:]

    top, bottom = pl.ds(0, 512), pl.ds(512, 512)
    zs = (other, z)

    def encode(slot, value):
        exponents = []
        for k in range(8):
            part = value[k * TILE : (k + 1) * TILE]
            largest = jnp.max(jnp.abs(part), axis=0, keepdims=True)
            exponent = jnp.floor(jnp.log2(jnp.maximum(largest, 1e-30))) + 1.0
            whole = jnp.floor(part * (32000.0 * jnp.exp2(-exponent)) + 0.5)
            slot[pl.ds(k * TILE, TILE), :] = whole.astype(jnp.int32).astype(jnp.int16)
            exponents.append(exponent)
        tail = jnp.concatenate(exponents + [jnp.zeros((8, 128), F32)], axis=0)
        slot[pl.ds(512, 16), :] = tail.astype(jnp.int32).astype(jnp.int16)

    def decoded(slot):
        scale = jnp.exp2(slot[pl.ds(512, 16), :].astype(jnp.int32).astype(F32)) * (1.0 / 32000.0)
        return jnp.concatenate(
            [
                slot[pl.ds(k * TILE, TILE), :].astype(jnp.int32).astype(F32) * scale[k : k + 1]
                for k in range(8)
            ],
            axis=0,
        )

    def rs_push(value, direction, kind, zi):
        k = (direction * 3 + kind) * 2 + zi
        src = sx.at[direction, kind, zi]
        encode(src, value)
        push(src, rx.at[direction, kind, zi], rs_send.at[k], rs_recv.at[k], (right, left)[direction])

    def rs_wait(direction, kind, zi):
        k = (direction * 3 + kind) * 2 + zi
        slot = rx.at[direction, kind, zi]
        remote(slot, slot, rs_send.at[k], rs_recv.at[k], sib).wait_recv()
        return decoded(slot)

    def rs_first(zi):
        rs_push(q[2, zs[zi], top, :], 0, 0, zi)
        rs_push(q[2, zs[zi], bottom, :], 1, 0, zi)

    def rs_direct(zi):
        rs_push(q[1, zs[zi], bottom, :], 0, 1, zi)
        rs_push(q[3, zs[zi], top, :], 1, 1, zi)

    def rs_second(zi):
        rs_push(q[1, zs[zi], top, :] + rs_wait(0, 0, zi), 0, 2, zi)
        rs_push(q[3, zs[zi], bottom, :] + rs_wait(1, 0, zi), 1, 2, zi)

    def take(ref, k, sib_k):
        arrived(ref, ag_send, ag_recv, k)
        push_same(ref, sib_send, sib_recv, sib_k, sib)

    share(2)
    share(1)
    take(block(xl, z, c), 0, 1)
    push_same(pair(xl, z, c, 0), ag_send, ag_recv, 3, right)
    push_same(half(xl, z, c, 1), ag_send, ag_recv, 5, zdev)
    take(block(xr, z, c), 1, 2)
    push_same(pair(xr, z, c, 1), ag_send, ag_recv, 4, left)
    push_same(half(xr, z, c, 1), ag_send, ag_recv, 6, zdev)
    take(block(x, other, c), 2, 3)
    push_same(half(x, other, c, 0), ag_send, ag_recv, 9, right)
    push_same(half(x, other, c, 0), ag_send, ag_recv, 10, left)
    rs_first(0)
    share(3)
    rs_direct(0)
    share(0)
    rs_first(1)
    rs_direct(1)

    loads[13].wait()

    def unit(x_, z_):
        u = x_ * 2 + z_
        cols = pl.ds(pl.multiple_of(u * 256, 256), 256)
        both = jnp.concatenate([acts[2 * u].reshape(1024, 128), acts[2 * u + 1].reshape(1024, 128)], axis=1)
        gtmp[...] = jnp.dot(got[...], both, preferred_element_type=F32)

        @pl.loop(0, 7)
        def _(k):
            rows = pl.ds(pl.multiple_of(k * TILE, TILE), TILE)
            kept = decay_rate * mom[rows, cols] + gtmp[rows, :]
            gtmp[rows, :] = kept
            scaled = kept * basis[pl.ds(k, 1), cols]
            high = scaled.astype(BF16)
            low = (scaled - high.astype(F32)).astype(BF16)
            ycat[rows, :] = jnp.concatenate([high, low], axis=1)

        ptmp[...] = jnp.dot(ycat[...], segments[...], preferred_element_type=F32)
        lines = lax.dot_general(chooser, ycat[...], (((1,), (1,)), ((), ())), preferred_element_type=F32)
        for s_ in range(4):
            p_own[z_, pl.ds(x_ * 4 + s_, 1), :] = lines[s_ : s_ + 1]

        @pl.loop(0, 7)
        def _(k):
            rows = pl.ds(pl.multiple_of(k * TILE, TILE), TILE)
            mom[rows, cols] = gtmp[rows, :] - ptmp[rows, :] * basis[pl.ds(k, 1), cols]

        copy = pltpu.make_async_copy(mom.at[:, cols], mo_hbm.at[:, cols], store_sem.at[len(stores)])
        copy.start()
        stores.append(copy)

    stores = []
    sb = lambda x_, z_: block(x_, z_, 1 - c)
    sh = lambda x_, z_, h: half(x_, z_, 1 - c, h)

    def from_sib(ref, k):
        arrived(ref, sib_send, sib_recv, k)

    def p_zh(group, z_):
        rows = pl.ds(pl.multiple_of(z_ * 16, 16), 16)
        p_all[zh, y, rows, :] = p_own[z_]
        mine = p_all.at[zh, y, rows]
        for k, dev in enumerate(zh_devs):
            push(mine, mine, ps_send.at[group, k], ps_recv.at[group, k], dev)

    def p_y(group, z_):
        rows = pl.ds(pl.multiple_of(z_ * 16, 16), 16)
        for k in range(3):
            slot = p_all.at[(zh + 3 - k) % 4, y, rows]
            remote(slot, slot, ps_send.at[group, k], ps_recv.at[group, k], sib).wait_recv()
        mine = p_all.at[:, y, rows]
        for k, dev in enumerate(y_devs):
            push(mine, mine, py_send.at[group, k], py_recv.at[group, k], dev)

    def p_done(group, z_):
        rows = pl.ds(pl.multiple_of(z_ * 16, 16), 16)
        for k in range(3):
            slot = p_all.at[:, (y + 3 - k) % 4, rows]
            remote(slot, slot, py_send.at[group, k], py_recv.at[group, k], sib).wait_recv()

    def decode(z_):
        for h in range(2):
            tiles = p_all[:, :, pl.ds(pl.multiple_of(z_ * 16 + h * 8, 8), 8), :].reshape(8, 2, 8, 448)
            even, odd = tiles[:, 0], tiles[:, 1]
            lines = jnp.concatenate(
                [
                    jnp.concatenate([even[:, rows], odd[:, rows]], axis=1).reshape(TILE, 448)
                    for rows in (slice(0, 4), slice(4, 8))
                ],
                axis=0,
            )
            turned = jnp.transpose(lines)
            high = turned.astype(BF16)
            low = (turned - high.astype(F32)).astype(BF16)
            for k in range(2):
                own_lanes = slice(k * TILE, (k + 1) * TILE)
                lhs[k] = jnp.concatenate([high[:, own_lanes], low[:, own_lanes], high[:, own_lanes]], axis=1)
                u = (h * 2 + k) * 2 + z_
                cols = pl.ds(pl.multiple_of(u * 256, 256), 256)
                for j in range(7):
                    rows = pl.ds(j * TILE, TILE)
                    terms = right_side[u, j]
                    full = jnp.concatenate([terms[:TILE], terms], axis=0)
                    upd[rows, cols] = jnp.dot(lhs[k, rows, :], full, preferred_element_type=F32).astype(BF16)

                copy = pltpu.make_async_copy(upd.at[:, cols], up_hbm.at[:, cols], store_sem.at[len(stores)])
                copy.start()
                stores.append(copy)

    from_sib(sb(x, z), 0)
    unit(x, z)
    for k, dev_k in ((0, 3), (1, 4)):
        take(pair(xo, z, c, k), dev_k, 4 + k)
        push_same(quarter(xo, z, c, 1, k), ag_send, ag_recv, 7 + k, zdev)
    take(half(xl, other, c, 0), 9, 6)
    push_same(quarter(xl, other, c, 0, 0), ag_send, ag_recv, 11, right)
    take(half(xr, other, c, 0), 10, 7)
    push_same(quarter(xr, other, c, 0, 1), ag_send, ag_recv, 12, left)
    from_sib(sb(xl, z), 1)
    unit(xl, z)
    from_sib(sb(xr, z), 2)
    unit(xr, z)
    take(half(xl, other, c, 1), 5, 8)
    take(half(xr, other, c, 1), 6, 9)
    for k in range(2):
        from_sib(pair(xo, z, 1 - c, k), 4 + k)
    unit(xo, z)
    p_zh(0, z)
    rs_second(0)
    from_sib(sb(x, other), 3)
    unit(x, other)
    for k in range(2):
        take(quarter(xo, other, c, 0, k), 11 + k, 10 + k)
        take(quarter(xo, other, c, 1, k), 7 + k, 12 + k)
    from_sib(sh(xl, other, 0), 6)
    from_sib(sh(xl, other, 1), 8)
    unit(xl, other)
    p_y(0, z)
    from_sib(sh(xr, other, 0), 7)
    from_sib(sh(xr, other, 1), 9)
    unit(xr, other)
    for k in range(2):
        from_sib(quarter(xo, other, 1 - c, 0, k), 10 + k)
        from_sib(quarter(xo, other, 1 - c, 1, k), 12 + k)
    unit(xo, other)
    p_zh(1, other)
    rs_second(1)

    def x_sum(zi):
        return (
            q[0, zs[zi], top, :] + rs_wait(0, 2, zi) + rs_wait(1, 1, zi),
            q[0, zs[zi], bottom, :] + rs_wait(0, 1, zi) + rs_wait(1, 2, zi),
        )

    for k, value in enumerate(x_sum(0)):
        encode(sz.at[k], value)
    push(sz, rz, zs_send, zs_recv, zdev)
    p_y(1, other)
    p_done(0, z)
    decode(z)
    p_done(1, other)
    decode(other)

    sums = x_sum(1)
    remote(sz, rz, zs_send, zs_recv, zdev).wait_recv()
    for k in range(2):
        ig[pl.ds(k * 512, 512), :] = (sums[k] + decoded(rz.at[k])).astype(BF16)
    last = pltpu.make_async_copy(ig, ig_hbm, store_sem.at[len(stores)])
    last.start()
    for copy in stores:
        copy.wait()
    last.wait()
    for copy in sent:
        copy.wait_send()


def body(activations, grad_out, weight, momentum, freq_rows):
    hbm = pl.BlockSpec(memory_space=pltpu.HBM)
    dma = pltpu.SemaphoreType.DMA
    table, terms = cosine_tables()
    input_grad, momentum_out, update = pl.pallas_call(
        kernel,
        out_shape=(
            jax.ShapeDtypeStruct((1024, 128), BF16),
            jax.ShapeDtypeStruct((448, 2048), F32),
            jax.ShapeDtypeStruct((448, 2048), BF16),
        ),
        in_specs=[hbm] * 7,
        out_specs=(hbm, hbm, hbm),
        scratch_shapes=[
            pltpu.VMEM((16, 2, 2, 256, 128), BF16),
            pltpu.VMEM((448, 1024), BF16),
            pltpu.VMEM((2, 1024, 448), BF16),
            pltpu.VMEM((2, 8, 448, 128), BF16),
            pltpu.VMEM((4, 2, 1024, 128), F32),
            pltpu.VMEM((2, 3, 2, 528, 128), jnp.int16),
            pltpu.VMEM((2, 3, 2, 528, 128), jnp.int16),
            pltpu.VMEM((2, 528, 128), jnp.int16),
            pltpu.VMEM((2, 528, 128), jnp.int16),
            pltpu.VMEM((448, 2048), F32),
            pltpu.VMEM((448, 256), F32),
            pltpu.VMEM((448, 256), F32),
            pltpu.VMEM((448, 512), BF16),
            pltpu.VMEM((7, 2048), F32),
            pltpu.VMEM((512, 256), BF16),
            pltpu.VMEM((8, 7, 128, 256), BF16),
            pltpu.VMEM((2, 448, 192), BF16),
            pltpu.VMEM((2, 16, 448), F32),
            pltpu.VMEM((4, 4, 32, 448), F32),
            pltpu.VMEM((448, 2048), BF16),
            pltpu.VMEM((1024, 128), BF16),
            pltpu.VMEM((7, 16, 32), jnp.int32),
            pltpu.VMEM((TILE, 128), F32),
            pltpu.VMEM((TILE, 512), BF16),
            dma((14,)), dma((17,)),
            dma((9,)), dma((9,)),
            dma((13,)), dma((13,)),
            dma((14,)), dma((14,)),
            dma((12,)), dma((12,)),
            dma, dma,
            dma((2, 3)), dma((2, 3)),
            dma((2, 3)), dma((2, 3)),
        ],
        compiler_params=pltpu.CompilerParams(
            collective_id=0, has_side_effects=True, vmem_limit_bytes=63 * 1024 * 1024
        ),
        name="demo_step",
    )(
        activations.reshape(2, 2, 256, 128),
        grad_out.T,
        weight.T,
        momentum[0].T,
        freq_rows.transpose(2, 0, 1),
        jnp.asarray(table),
        jnp.asarray(terms),
    )
    return input_grad, momentum_out.T[None], update.T


def solution(mesh):
    placed = (
        P("replica", "tensor"),
        P("replica", "tensor"),
        P(None, "tensor"),
        P("replica", None, "tensor"),
        P(None, None, "tensor"),
    )
    return jax.shard_map(
        body,
        mesh=mesh,
        in_specs=placed,
        out_specs=(P("replica", "tensor"), P("replica", None, "tensor"), P(None, "tensor")),
        check_vma=False,
    )
```

```python
import functools

import jax
import jax.numpy as jnp
import numpy as np
from jax import lax
from jax.experimental import pallas as pl
from jax.experimental.pallas import tpu as pltpu
from jax.sharding import PartitionSpec as P

MESH = pl.DeviceIdType.MESH
F32 = jnp.float32
BF16 = jnp.bfloat16

TILE = 64
decay_rate = 0.9


def cosine_tables():
    freq = np.arange(TILE, dtype=np.float64)[:, None]
    place = np.arange(TILE, dtype=np.float64)[None, :]
    values = np.cos(np.pi * (2.0 * place + 1.0) * freq / (2.0 * TILE)) * np.sqrt(2.0 / TILE)
    values = np.where(freq == 0.0, values / np.sqrt(2.0), values).astype(np.float32)
    high = values.astype(BF16)
    low = (values - high.astype(np.float32)).astype(BF16)
    return np.concatenate([values] * 2, axis=1), np.concatenate([high] * 4 + [low] * 4, axis=1)


def kernel(
    act_hbm, go_hbm, w_hbm, mom_hbm, freq_hbm, cos_hbm, terms_hbm,
    ig, mom, upd,
    acts, got, go, wt, q, sx, rx, sz, rz, gtmp, ptmp, ycat, basis, segments, right_side, lhs, p_own, p_all,
    freq_ref, cos_ref, terms_ref,
    load_sem, ex_send, ex_recv, ag_send, ag_recv, sib_send, sib_recv,
    rs_send, rs_recv, zs_send, zs_recv, ps_send, ps_recv, py_send, py_recv,
):
    r = lax.axis_index("replica")
    t = lax.axis_index("tensor")
    x, z, c = t // 4, (t // 2) % 2, t % 2
    zh, y = r // 4, r % 4
    other = 1 - z

    def at(x_, z_, c_):
        return (r, x_ * 4 + z_ * 2 + c_)

    xr, xl, xo = (x + 1) % 4, (x + 3) % 4, (x + 2) % 4
    right, left = at(xr, z, c), at(xl, z, c)
    zdev, sib = at(x, other, c), at(x, z, 1 - c)
    zh_devs = [(((zh + k) % 4) * 4 + y, t) for k in (1, 2, 3)]
    y_devs = [(zh * 4 + (y + k) % 4, t) for k in (1, 2, 3)]

    def w_cols(u, c_):
        return w_hbm.at[:, pl.ds(pl.multiple_of((2 * u + c_) * 128, 128), 128)]

    loads = [
        pltpu.make_async_copy(go_hbm, got, load_sem.at[0]),
        pltpu.make_async_copy(act_hbm, acts.at[t], load_sem.at[1]),
        pltpu.make_async_copy(freq_hbm, freq_ref, load_sem.at[2]),
        pltpu.make_async_copy(cos_hbm, cos_ref, load_sem.at[3]),
        pltpu.make_async_copy(terms_hbm, terms_ref, load_sem.at[4]),
    ] + [pltpu.make_async_copy(w_cols(u, c), wt.at[0, u], load_sem.at[5 + u]) for u in range(8)]
    loads.append(pltpu.make_async_copy(mom_hbm, mom, load_sem.at[13]))
    for load in loads:
        load.start()

    barrier = pltpu.get_barrier_semaphore()
    peers = [right, left, zdev, sib] + zh_devs + y_devs
    for peer in peers:
        pl.semaphore_signal(barrier, inc=1, device_id=peer, device_id_type=MESH)

    loads[0].wait()
    go[0] = jnp.transpose(got[...])
    loads[1].wait()
    pl.semaphore_wait(barrier, len(peers))

    def remote(src, dst, send, recv, dev):
        return pltpu.make_async_remote_copy(
            src_ref=src, dst_ref=dst, send_sem=send, recv_sem=recv, device_id=dev, device_id_type=MESH
        )

    sent = []

    def push(src, dst, send, recv, dev):
        copy = remote(src, dst, send, recv, dev)
        copy.start()
        sent.append(copy)

    def block(x_, z_, c_):
        return acts.at[x_ * 4 + z_ * 2 + c_]

    def half(x_, z_, c_, h):
        return acts.at[x_ * 4 + z_ * 2 + c_, h]

    def quarter(x_, z_, c_, h, k):
        return acts.at[x_ * 4 + z_ * 2 + c_, h, k]

    def push_same(ref, sends, recvs, k, dev):
        push(ref, ref, sends.at[k], recvs.at[k], dev)

    def arrived(ref, sends, recvs, k):
        remote(ref, ref, sends.at[k], recvs.at[k], sib).wait_recv()

    def own(h):
        return half(x, z, c, h)

    push_same(own(1), ag_send, ag_recv, 0, right)
    push_same(own(1), ag_send, ag_recv, 1, left)
    push_same(own(0), ag_send, ag_recv, 2, zdev)
    push_same(own(0), ag_send, ag_recv, 3, right)
    push_same(own(0), ag_send, ag_recv, 4, left)
    push_same(own(1), ag_send, ag_recv, 5, zdev)
    push(go.at[0], go.at[1], ex_send.at[0], ex_recv.at[0], sib)
    for u in range(8):
        push(w_cols(u, 1 - c), wt.at[1, u], ex_send.at[1 + u], ex_recv.at[1 + u], sib)
    push_same(block(x, z, c), sib_send, sib_recv, 0, sib)

    for load in loads[2:5]:
        load.wait()

    mine = jnp.concatenate([freq_ref[k, pl.ds(r, 1), :] for k in range(7)], axis=0)
    first = lax.broadcasted_iota(jnp.int32, (7, 128), 1) < TILE
    spread = jnp.concatenate(
        [jnp.where(first, mine[:, 2 * k : 2 * k + 1], mine[:, 2 * k + 1 : 2 * k + 2]) for k in range(16)], axis=1
    )

    def pick(k, so_far):
        row = jnp.concatenate([cos_ref[pl.ds(k, 1), :]] * 16, axis=1)
        return jnp.where(spread == k, row, so_far)

    basis[...] = lax.fori_loop(0, TILE, pick, jnp.zeros((7, 2048), F32))

    segments[...] = (
        lax.broadcasted_iota(jnp.int32, (512, 256), 0) % 256 // TILE
        == lax.broadcasted_iota(jnp.int32, (512, 256), 1) // TILE
    ).astype(F32).astype(BF16)
    chooser = (
        lax.broadcasted_iota(jnp.int32, (8, 512), 1) % 256 // TILE
        == lax.broadcasted_iota(jnp.int32, (8, 512), 0)
    ).astype(F32).astype(BF16)

    widen = (
        lax.broadcasted_iota(jnp.int32, (TILE, 16), 0) // 4 == lax.broadcasted_iota(jnp.int32, (TILE, 16), 1)
    ).astype(F32).astype(BF16)
    wide = jnp.concatenate(
        [jnp.dot(widen, freq_ref[k].astype(F32).astype(BF16), preferred_element_type=F32) for k in range(7)], axis=0
    )
    keep = (
        lax.broadcasted_iota(jnp.int32, (448, 32), 0) % 4 == lax.broadcasted_iota(jnp.int32, (448, 32), 1) % 4
    )
    narrow = (
        lax.broadcasted_iota(jnp.int32, (32, 8), 0) // 4 == lax.broadcasted_iota(jnp.int32, (32, 8), 1)
    ).astype(F32).astype(BF16)
    columns = jnp.dot(jnp.where(keep, wide, 0.0).astype(BF16), narrow, preferred_element_type=F32)
    freq_lane = lax.broadcasted_iota(jnp.int32, (448, TILE), 1).astype(F32)
    same = (
        lax.broadcasted_iota(jnp.int32, (TILE, 256), 0) % 4 == lax.broadcasted_iota(jnp.int32, (TILE, 256), 1) // TILE
    )
    for u in range(8):
        hot = (columns[:, u : u + 1] == freq_lane).astype(F32).astype(BF16)
        both = jnp.dot(hot, terms_ref[...], preferred_element_type=F32)
        for k in range(7):
            rows = both[k * TILE : (k + 1) * TILE]
            right_side[u, k, pl.ds(0, TILE), :] = jnp.where(same, rows[:, :256], 0.0).astype(BF16)
            right_side[u, k, pl.ds(TILE, TILE), :] = jnp.where(same, rows[:, 256:], 0.0).astype(BF16)

    def take(ref, k, sib_k):
        arrived(ref, ag_send, ag_recv, k)
        push_same(ref, sib_send, sib_recv, sib_k, sib)

    take(half(xl, z, c, 1), 0, 1)
    push_same(half(xl, z, c, 1), ag_send, ag_recv, 6, zdev)
    push_same(quarter(xl, z, c, 1, 0), ag_send, ag_recv, 7, right)
    take(half(xr, z, c, 1), 1, 2)
    push_same(half(xr, z, c, 1), ag_send, ag_recv, 8, zdev)
    push_same(quarter(xr, z, c, 1, 1), ag_send, ag_recv, 9, left)
    take(half(x, other, c, 0), 2, 3)
    push_same(half(x, other, c, 0), ag_send, ag_recv, 10, right)
    push_same(half(x, other, c, 0), ag_send, ag_recv, 11, left)

    for load in loads[5:13]:
        load.wait()
    remote(go.at[0], go.at[1], ex_send.at[0], ex_recv.at[0], sib).wait_recv()
    for u in range(8):
        remote(wt.at[0, u], wt.at[1, u], ex_send.at[1 + u], ex_recv.at[1 + u], sib).wait_recv()

    def share(dx):
        dest = (x + dx) % 4

        @pl.loop(0, 4)
        def _(k):
            rows = pl.ds(pl.multiple_of(k * 256, 256), 256)
            total = jnp.zeros((256, 256), F32)
            for part in range(2):
                pair = jnp.concatenate([wt[part, dest * 2], wt[part, dest * 2 + 1]], axis=1)
                total += jnp.dot(go[part, rows, :], pair, preferred_element_type=F32)
            q[dx, 0, rows, :] = total[:, :128]
            q[dx, 1, rows, :] = total[:, 128:]

    top, bottom = pl.ds(0, 512), pl.ds(512, 512)
    zs = (other, z)

    def encode(slot, value):
        exponents = []
        for k in range(8):
            part = value[k * TILE : (k + 1) * TILE]
            largest = jnp.max(jnp.abs(part), axis=0, keepdims=True)
            exponent = jnp.floor(jnp.log2(jnp.maximum(largest, 1e-30))) + 1.0
            whole = jnp.floor(part * (32000.0 * jnp.exp2(-exponent)) + 0.5)
            slot[pl.ds(k * TILE, TILE), :] = whole.astype(jnp.int32).astype(jnp.int16)
            exponents.append(exponent)
        tail = jnp.concatenate(exponents + [jnp.zeros((8, 128), F32)], axis=0)
        slot[pl.ds(512, 16), :] = tail.astype(jnp.int32).astype(jnp.int16)

    def decoded(slot):
        scale = jnp.exp2(slot[pl.ds(512, 16), :].astype(jnp.int32).astype(F32)) * (1.0 / 32000.0)
        return jnp.concatenate(
            [
                slot[pl.ds(k * TILE, TILE), :].astype(jnp.int32).astype(F32) * scale[k : k + 1]
                for k in range(8)
            ],
            axis=0,
        )

    def rs_push(value, direction, kind, zi):
        k = (direction * 3 + kind) * 2 + zi
        src = sx.at[direction, kind, zi]
        encode(src, value)
        push(src, rx.at[direction, kind, zi], rs_send.at[k], rs_recv.at[k], (right, left)[direction])

    def rs_wait(direction, kind, zi):
        k = (direction * 3 + kind) * 2 + zi
        slot = rx.at[direction, kind, zi]
        remote(slot, slot, rs_send.at[k], rs_recv.at[k], sib).wait_recv()
        return decoded(slot)

    def rs_first(zi):
        rs_push(q[2, zs[zi], top, :], 0, 0, zi)
        rs_push(q[2, zs[zi], bottom, :], 1, 0, zi)

    def rs_direct(zi):
        rs_push(q[1, zs[zi], bottom, :], 0, 1, zi)
        rs_push(q[3, zs[zi], top, :], 1, 1, zi)

    def rs_second(zi):
        rs_push(q[1, zs[zi], top, :] + rs_wait(0, 0, zi), 0, 2, zi)
        rs_push(q[3, zs[zi], bottom, :] + rs_wait(1, 0, zi), 1, 2, zi)

    share(2)
    take(half(xl, z, c, 0), 3, 4)
    push_same(quarter(xl, z, c, 0, 0), ag_send, ag_recv, 12, right)
    take(half(xr, z, c, 0), 4, 5)
    push_same(quarter(xr, z, c, 0, 1), ag_send, ag_recv, 13, left)
    take(half(x, other, c, 1), 5, 6)
    rs_first(0)
    share(1)
    share(3)
    take(quarter(xo, z, c, 1, 0), 7, 7)
    push_same(quarter(xo, z, c, 1, 0), ag_send, ag_recv, 14, zdev)
    take(quarter(xo, z, c, 1, 1), 9, 8)
    push_same(quarter(xo, z, c, 1, 1), ag_send, ag_recv, 15, zdev)
    take(half(xl, other, c, 0), 10, 9)
    push_same(quarter(xl, other, c, 0, 0), ag_send, ag_recv, 16, right)
    take(half(xr, other, c, 0), 11, 10)
    push_same(quarter(xr, other, c, 0, 1), ag_send, ag_recv, 17, left)
    rs_direct(0)
    share(0)
    rs_first(1)
    rs_direct(1)

    loads[13].wait()

    def unit(dx, x_, z_, zi):
        u = x_ * 2 + z_
        cols = pl.ds(pl.multiple_of(u * 256, 256), 256)
        both = jnp.concatenate([acts[2 * u].reshape(1024, 128), acts[2 * u + 1].reshape(1024, 128)], axis=1)
        gtmp[...] = jnp.dot(got[...], both, preferred_element_type=F32)

        for k in range(7):
            rows = pl.ds(k * TILE, TILE)
            kept = decay_rate * mom[rows, cols] + gtmp[rows, :]
            gtmp[rows, :] = kept
            scaled = kept * basis[k : k + 1, cols]
            high = scaled.astype(BF16)
            low = (scaled - high.astype(F32)).astype(BF16)
            ycat[rows, :] = jnp.concatenate([high, low], axis=1)

        ptmp[...] = jnp.dot(ycat[...], segments[...], preferred_element_type=F32)
        lines = lax.dot_general(chooser, ycat[...], (((1,), (1,)), ((), ())), preferred_element_type=F32)
        p_own[zi, dx // 2, pl.ds(dx % 2 * 4, 4), :] = lines[:4]
        for k in range(7):
            rows = pl.ds(k * TILE, TILE)
            mom[rows, cols] = gtmp[rows, :] - ptmp[rows, :] * basis[k : k + 1, cols]

    sb = lambda x_, z_: block(x_, z_, 1 - c)
    sh = lambda x_, z_, h: half(x_, z_, 1 - c, h)

    def from_sib(ref, k):
        arrived(ref, sib_send, sib_recv, k)

    xs = (x, xl, xr, xo)

    def p_zh(group):
        p_all[group, zh, y] = p_own[group // 2, group % 2]
        mine = p_all.at[group, zh, y]
        for k, dev in enumerate(zh_devs):
            push(mine, mine, ps_send.at[group, k], ps_recv.at[group, k], dev)

    def p_y(group):
        for k in range(3):
            slot = p_all.at[group, (zh + 3 - k) % 4, y]
            remote(slot, slot, ps_send.at[group, k], ps_recv.at[group, k], sib).wait_recv()
        mine = p_all.at[group, :, y]
        for k, dev in enumerate(y_devs):
            push(mine, mine, py_send.at[group, k], py_recv.at[group, k], dev)

    def finish(group):
        for k in range(3):
            slot = p_all.at[group, :, (y + 3 - k) % 4]
            remote(slot, slot, py_send.at[group, k], py_recv.at[group, k], sib).wait_recv()
        tiles = p_all[group].reshape(8, 2, 8, 448)
        even, odd = tiles[:, 0], tiles[:, 1]
        lines = jnp.concatenate(
            [
                jnp.concatenate([even[:, rows], odd[:, rows]], axis=1).reshape(TILE, 448)
                for rows in (slice(0, 4), slice(4, 8))
            ],
            axis=0,
        )
        turned = jnp.transpose(lines)
        high = turned.astype(BF16)
        low = (turned - high.astype(F32)).astype(BF16)
        for k in range(2):
            own_lanes = slice(k * TILE, (k + 1) * TILE)
            lhs[k] = jnp.concatenate([high[:, own_lanes], low[:, own_lanes], high[:, own_lanes]], axis=1)
            u = xs[group % 2 * 2 + k] * 2 + (z, other)[group // 2]
            cols = pl.ds(pl.multiple_of(u * 256, 256), 256)
            for j in range(7):
                rows = pl.ds(j * TILE, TILE)
                terms = right_side[u, j]
                full = jnp.concatenate([terms[:TILE], terms], axis=0)
                upd[rows, cols] = jnp.dot(lhs[k, rows, :], full, preferred_element_type=F32).astype(BF16)

    from_sib(sb(x, z), 0)
    unit(0, x, z, 0)
    from_sib(sh(xl, z, 1), 1)
    from_sib(sh(xl, z, 0), 4)
    unit(1, xl, z, 0)
    p_zh(0)
    take(quarter(xo, z, c, 0, 0), 12, 11)
    take(quarter(xo, z, c, 0, 1), 13, 12)
    take(half(xl, other, c, 1), 6, 13)
    take(half(xr, other, c, 1), 8, 14)
    from_sib(sh(xr, z, 1), 2)
    from_sib(sh(xr, z, 0), 5)
    unit(2, xr, z, 0)
    from_sib(quarter(xo, z, 1 - c, 1, 0), 7)
    from_sib(quarter(xo, z, 1 - c, 1, 1), 8)
    from_sib(quarter(xo, z, 1 - c, 0, 0), 11)
    from_sib(quarter(xo, z, 1 - c, 0, 1), 12)
    unit(3, xo, z, 0)
    p_zh(1)
    rs_second(0)
    from_sib(sh(x, other, 0), 3)
    from_sib(sh(x, other, 1), 6)
    unit(0, x, other, 1)
    take(quarter(xo, other, c, 0, 0), 16, 15)
    take(quarter(xo, other, c, 0, 1), 17, 16)
    take(quarter(xo, other, c, 1, 0), 14, 17)
    take(quarter(xo, other, c, 1, 1), 15, 18)
    p_y(0)
    from_sib(sh(xl, other, 0), 9)
    from_sib(sh(xl, other, 1), 13)
    unit(1, xl, other, 1)
    p_zh(2)
    p_y(1)
    from_sib(sh(xr, other, 0), 10)
    from_sib(sh(xr, other, 1), 14)
    unit(2, xr, other, 1)
    from_sib(quarter(xo, other, 1 - c, 0, 0), 15)
    from_sib(quarter(xo, other, 1 - c, 0, 1), 16)
    from_sib(quarter(xo, other, 1 - c, 1, 0), 17)
    from_sib(quarter(xo, other, 1 - c, 1, 1), 18)
    unit(3, xo, other, 1)
    p_zh(3)
    rs_second(1)
    p_y(2)

    def x_sum(zi):
        return (
            q[0, zs[zi], top, :] + rs_wait(0, 2, zi) + rs_wait(1, 1, zi),
            q[0, zs[zi], bottom, :] + rs_wait(0, 1, zi) + rs_wait(1, 2, zi),
        )

    for k, value in enumerate(x_sum(0)):
        encode(sz.at[k], value)
    push(sz, rz, zs_send, zs_recv, zdev)
    finish(0)
    p_y(3)
    finish(1)
    finish(2)
    finish(3)

    sums = x_sum(1)
    remote(sz, rz, zs_send, zs_recv, zdev).wait_recv()
    for k in range(2):
        ig[pl.ds(k * 512, 512), :] = (sums[k] + decoded(rz.at[k])).astype(BF16)
    for copy in sent:
        copy.wait_send()


def store(*refs):
    sources, targets, sems = refs[:3], refs[3:6], refs[6]
    copies = []
    for k, (source, target) in enumerate(zip(sources, targets)):
        height = source.shape[0] // 4
        for part in range(4):
            rows = pl.ds(part * height, height)
            copies.append(pltpu.make_async_copy(source.at[rows], target.at[rows], sems.at[k, part]))
    for copy in copies:
        copy.start()
    for copy in copies:
        copy.wait()


def body(activations, grad_out, weight, momentum, freq_rows):
    hbm = pl.BlockSpec(memory_space=pltpu.HBM)
    vmem = pl.BlockSpec(memory_space=pltpu.VMEM)
    dma = pltpu.SemaphoreType.DMA
    outs = (
        jax.ShapeDtypeStruct((1024, 128), BF16),
        jax.ShapeDtypeStruct((448, 2048), F32),
        jax.ShapeDtypeStruct((448, 2048), BF16),
    )
    table, terms = cosine_tables()
    input_grad, momentum_out, update = pl.pallas_call(
        kernel,
        out_shape=outs,
        in_specs=[hbm] * 7,
        out_specs=(vmem, vmem, vmem),
        scratch_shapes=[
            pltpu.VMEM((16, 2, 2, 256, 128), BF16),
            pltpu.VMEM((448, 1024), BF16),
            pltpu.VMEM((2, 1024, 448), BF16),
            pltpu.VMEM((2, 8, 448, 128), BF16),
            pltpu.VMEM((4, 2, 1024, 128), F32),
            pltpu.VMEM((2, 3, 2, 528, 128), jnp.int16),
            pltpu.VMEM((2, 3, 2, 528, 128), jnp.int16),
            pltpu.VMEM((2, 528, 128), jnp.int16),
            pltpu.VMEM((2, 528, 128), jnp.int16),
            pltpu.VMEM((448, 256), F32),
            pltpu.VMEM((448, 256), F32),
            pltpu.VMEM((448, 512), BF16),
            pltpu.VMEM((7, 2048), F32),
            pltpu.VMEM((512, 256), BF16),
            pltpu.VMEM((8, 7, 128, 256), BF16),
            pltpu.VMEM((2, 448, 192), BF16),
            pltpu.VMEM((2, 2, 8, 448), F32),
            pltpu.VMEM((4, 4, 4, 8, 448), F32),
            pltpu.VMEM((7, 16, 32), jnp.int32),
            pltpu.VMEM((TILE, 128), F32),
            pltpu.VMEM((TILE, 512), BF16),
            dma((14,)),
            dma((9,)), dma((9,)),
            dma((18,)), dma((18,)),
            dma((19,)), dma((19,)),
            dma((12,)), dma((12,)),
            dma, dma,
            dma((4, 3)), dma((4, 3)),
            dma((4, 3)), dma((4, 3)),
        ],
        compiler_params=pltpu.CompilerParams(
            collective_id=0, has_side_effects=True, vmem_limit_bytes=40 * 1024 * 1024
        ),
        name="demo_step",
    )(
        *(
            pltpu.with_memory_space_constraint(value, pltpu.HBM)
            for value in (
                activations.reshape(2, 2, 256, 128),
                grad_out.T,
                weight.T,
                momentum[0].T,
                freq_rows.transpose(2, 0, 1),
                jnp.asarray(table),
                jnp.asarray(terms),
            )
        )
    )
    input_grad, momentum_out, update = pl.pallas_call(
        store,
        out_shape=outs,
        in_specs=[pl.BlockSpec(memory_space=pl.ANY)] * 3,
        out_specs=(hbm, hbm, hbm),
        scratch_shapes=[dma((3, 4))],
        compiler_params=pltpu.CompilerParams(vmem_limit_bytes=4 * 1024 * 1024),
        name="store_results",
    )(*(pltpu.with_memory_space_constraint(value, pltpu.VMEM) for value in (input_grad, momentum_out, update)))
    return input_grad, momentum_out.T[None], update.T


def solution(mesh):
    placed = (
        P("replica", "tensor"),
        P("replica", "tensor"),
        P(None, "tensor"),
        P("replica", None, "tensor"),
        P(None, None, "tensor"),
    )
    return jax.shard_map(
        body,
        mesh=mesh,
        in_specs=placed,
        out_specs=(P("replica", "tensor"), P("replica", None, "tensor"), P(None, "tensor")),
        check_vma=False,
    )
```

```python
import functools

import jax
import jax.numpy as jnp
import numpy as np
from jax import lax
from jax.experimental import pallas as pl
from jax.experimental.pallas import tpu as pltpu
from jax.sharding import PartitionSpec as P

MESH = pl.DeviceIdType.MESH
F32 = jnp.float32
BF16 = jnp.bfloat16

TILE = 64
decay_rate = 0.9


def cosine_tables():
    freq = np.arange(TILE, dtype=np.float64)[:, None]
    place = np.arange(TILE, dtype=np.float64)[None, :]
    values = np.cos(np.pi * (2.0 * place + 1.0) * freq / (2.0 * TILE)) * np.sqrt(2.0 / TILE)
    values = np.where(freq == 0.0, values / np.sqrt(2.0), values).astype(np.float32)
    high = values.astype(BF16)
    low = (values - high.astype(np.float32)).astype(BF16)
    return np.concatenate([values] * 2, axis=1), np.concatenate([high] * 4 + [low] * 4, axis=1)


def kernel(
    act_hbm, go_hbm, w_hbm, mom_hbm, freq_hbm, cos_hbm, terms_hbm,
    ig, mom, upd,
    acts, got, go, wt, q, sx, rx, sz, rz, gtmp, ptmp, ycat, basis, segments, right_side, lhs, p_own, p_all,
    freq_ref, cos_ref, terms_ref,
    load_sem, ex_send, ex_recv, ag_send, ag_recv, sib_send, sib_recv,
    rs_send, rs_recv, zs_send, zs_recv, ps_send, ps_recv, py_send, py_recv,
):
    r = lax.axis_index("replica")
    t = lax.axis_index("tensor")
    x, z, c = t // 4, (t // 2) % 2, t % 2
    zh, y = r // 4, r % 4
    other = 1 - z

    def at(x_, z_, c_):
        return (r, x_ * 4 + z_ * 2 + c_)

    xr, xl, xo = (x + 1) % 4, (x + 3) % 4, (x + 2) % 4
    right, left = at(xr, z, c), at(xl, z, c)
    zdev, sib = at(x, other, c), at(x, z, 1 - c)
    zh_devs = [(((zh + k) % 4) * 4 + y, t) for k in (1, 2, 3)]
    y_devs = [(zh * 4 + (y + k) % 4, t) for k in (1, 2, 3)]

    def w_cols(u, c_):
        return w_hbm.at[:, pl.ds(pl.multiple_of((2 * u + c_) * 128, 128), 128)]

    loads = [
        pltpu.make_async_copy(go_hbm, got, load_sem.at[0]),
        pltpu.make_async_copy(act_hbm, acts.at[t], load_sem.at[1]),
        pltpu.make_async_copy(freq_hbm, freq_ref, load_sem.at[2]),
        pltpu.make_async_copy(cos_hbm, cos_ref, load_sem.at[3]),
        pltpu.make_async_copy(terms_hbm, terms_ref, load_sem.at[4]),
    ] + [pltpu.make_async_copy(w_cols(u, c), wt.at[0, u], load_sem.at[5 + u]) for u in range(8)]
    loads.append(pltpu.make_async_copy(mom_hbm, mom, load_sem.at[13]))
    for load in loads:
        load.start()

    barrier = pltpu.get_barrier_semaphore()
    peers = [right, left, zdev, sib] + zh_devs + y_devs
    for peer in peers:
        pl.semaphore_signal(barrier, inc=1, device_id=peer, device_id_type=MESH)

    loads[0].wait()
    go[0] = jnp.transpose(got[...])
    loads[1].wait()
    pl.semaphore_wait(barrier, len(peers))

    def remote(src, dst, send, recv, dev):
        return pltpu.make_async_remote_copy(
            src_ref=src, dst_ref=dst, send_sem=send, recv_sem=recv, device_id=dev, device_id_type=MESH
        )

    sent = []

    def push(src, dst, send, recv, dev):
        copy = remote(src, dst, send, recv, dev)
        copy.start()
        sent.append(copy)

    def block(x_, z_, c_):
        return acts.at[x_ * 4 + z_ * 2 + c_]

    def half(x_, z_, c_, h):
        return acts.at[x_ * 4 + z_ * 2 + c_, h]

    def quarter(x_, z_, c_, h, k):
        return acts.at[x_ * 4 + z_ * 2 + c_, h, k]

    def push_same(ref, sends, recvs, k, dev):
        push(ref, ref, sends.at[k], recvs.at[k], dev)

    def arrived(ref, sends, recvs, k):
        remote(ref, ref, sends.at[k], recvs.at[k], sib).wait_recv()

    def own(h):
        return half(x, z, c, h)

    push_same(own(1), ag_send, ag_recv, 0, right)
    push_same(own(1), ag_send, ag_recv, 1, left)
    push_same(own(0), ag_send, ag_recv, 2, zdev)
    push_same(own(0), ag_send, ag_recv, 3, right)
    push_same(own(0), ag_send, ag_recv, 4, left)
    push_same(own(1), ag_send, ag_recv, 5, zdev)
    push(go.at[0], go.at[1], ex_send.at[0], ex_recv.at[0], sib)
    for u in range(8):
        push(w_cols(u, 1 - c), wt.at[1, u], ex_send.at[1 + u], ex_recv.at[1 + u], sib)
    push_same(block(x, z, c), sib_send, sib_recv, 0, sib)

    for load in loads[2:5]:
        load.wait()

    mine = jnp.concatenate([freq_ref[k, pl.ds(r, 1), :] for k in range(7)], axis=0)
    first = lax.broadcasted_iota(jnp.int32, (7, 128), 1) < TILE
    spread = jnp.concatenate(
        [jnp.where(first, mine[:, 2 * k : 2 * k + 1], mine[:, 2 * k + 1 : 2 * k + 2]) for k in range(16)], axis=1
    )

    def pick(k, so_far):
        row = jnp.concatenate([cos_ref[pl.ds(k, 1), :]] * 16, axis=1)
        return jnp.where(spread == k, row, so_far)

    basis[...] = lax.fori_loop(0, TILE, pick, jnp.zeros((7, 2048), F32))

    segments[...] = (
        lax.broadcasted_iota(jnp.int32, (512, 256), 0) % 256 // TILE
        == lax.broadcasted_iota(jnp.int32, (512, 256), 1) // TILE
    ).astype(F32).astype(BF16)
    chooser = (
        lax.broadcasted_iota(jnp.int32, (8, 512), 1) % 256 // TILE
        == lax.broadcasted_iota(jnp.int32, (8, 512), 0)
    ).astype(F32).astype(BF16)

    widen = (
        lax.broadcasted_iota(jnp.int32, (TILE, 16), 0) // 4 == lax.broadcasted_iota(jnp.int32, (TILE, 16), 1)
    ).astype(F32).astype(BF16)
    wide = jnp.concatenate(
        [jnp.dot(widen, freq_ref[k].astype(F32).astype(BF16), preferred_element_type=F32) for k in range(7)], axis=0
    )
    keep = (
        lax.broadcasted_iota(jnp.int32, (448, 32), 0) % 4 == lax.broadcasted_iota(jnp.int32, (448, 32), 1) % 4
    )
    narrow = (
        lax.broadcasted_iota(jnp.int32, (32, 8), 0) // 4 == lax.broadcasted_iota(jnp.int32, (32, 8), 1)
    ).astype(F32).astype(BF16)
    columns = jnp.dot(jnp.where(keep, wide, 0.0).astype(BF16), narrow, preferred_element_type=F32)
    freq_lane = lax.broadcasted_iota(jnp.int32, (448, TILE), 1).astype(F32)
    same = (
        lax.broadcasted_iota(jnp.int32, (TILE, 256), 0) % 4 == lax.broadcasted_iota(jnp.int32, (TILE, 256), 1) // TILE
    )
    for u in range(8):
        hot = (columns[:, u : u + 1] == freq_lane).astype(F32).astype(BF16)
        both = jnp.dot(hot, terms_ref[...], preferred_element_type=F32)
        for k in range(7):
            rows = both[k * TILE : (k + 1) * TILE]
            right_side[u, k, pl.ds(0, TILE), :] = jnp.where(same, rows[:, :256], 0.0).astype(BF16)
            right_side[u, k, pl.ds(TILE, TILE), :] = jnp.where(same, rows[:, 256:], 0.0).astype(BF16)

    def take(ref, k, sib_k):
        arrived(ref, ag_send, ag_recv, k)
        push_same(ref, sib_send, sib_recv, sib_k, sib)

    take(half(xl, z, c, 1), 0, 1)
    push_same(half(xl, z, c, 1), ag_send, ag_recv, 6, zdev)
    push_same(quarter(xl, z, c, 1, 0), ag_send, ag_recv, 7, right)
    take(half(xr, z, c, 1), 1, 2)
    push_same(half(xr, z, c, 1), ag_send, ag_recv, 8, zdev)
    push_same(quarter(xr, z, c, 1, 1), ag_send, ag_recv, 9, left)
    take(half(x, other, c, 0), 2, 3)
    push_same(half(x, other, c, 0), ag_send, ag_recv, 10, right)
    push_same(half(x, other, c, 0), ag_send, ag_recv, 11, left)

    for load in loads[5:13]:
        load.wait()
    remote(go.at[0], go.at[1], ex_send.at[0], ex_recv.at[0], sib).wait_recv()
    for u in range(8):
        remote(wt.at[0, u], wt.at[1, u], ex_send.at[1 + u], ex_recv.at[1 + u], sib).wait_recv()

    def share(dx):
        dest = (x + dx) % 4

        @pl.loop(0, 4)
        def _(k):
            rows = pl.ds(pl.multiple_of(k * 256, 256), 256)
            total = jnp.zeros((256, 256), F32)
            for part in range(2):
                pair = jnp.concatenate([wt[part, dest * 2], wt[part, dest * 2 + 1]], axis=1)
                total += jnp.dot(go[part, rows, :], pair, preferred_element_type=F32)
            q[dx, 0, rows, :] = total[:, :128]
            q[dx, 1, rows, :] = total[:, 128:]

    top, bottom = pl.ds(0, 512), pl.ds(512, 512)
    zs = (other, z)

    def encode(slot, value):
        exponents = []
        for k in range(8):
            part = value[k * TILE : (k + 1) * TILE]
            largest = jnp.max(jnp.abs(part), axis=0, keepdims=True)
            exponent = jnp.floor(jnp.log2(jnp.maximum(largest, 1e-30))) + 1.0
            whole = jnp.floor(part * (32000.0 * jnp.exp2(-exponent)) + 0.5)
            slot[pl.ds(k * TILE, TILE), :] = whole.astype(jnp.int32).astype(jnp.int16)
            exponents.append(exponent)
        tail = jnp.concatenate(exponents + [jnp.zeros((8, 128), F32)], axis=0)
        slot[pl.ds(512, 16), :] = tail.astype(jnp.int32).astype(jnp.int16)

    def decoded(slot):
        scale = jnp.exp2(slot[pl.ds(512, 16), :].astype(jnp.int32).astype(F32)) * (1.0 / 32000.0)
        return jnp.concatenate(
            [
                slot[pl.ds(k * TILE, TILE), :].astype(jnp.int32).astype(F32) * scale[k : k + 1]
                for k in range(8)
            ],
            axis=0,
        )

    def rs_push(value, direction, kind, zi):
        k = (direction * 3 + kind) * 2 + zi
        src = sx.at[direction, kind, zi]
        encode(src, value)
        push(src, rx.at[direction, kind, zi], rs_send.at[k], rs_recv.at[k], (right, left)[direction])

    def rs_wait(direction, kind, zi):
        k = (direction * 3 + kind) * 2 + zi
        slot = rx.at[direction, kind, zi]
        remote(slot, slot, rs_send.at[k], rs_recv.at[k], sib).wait_recv()
        return decoded(slot)

    def rs_first(zi):
        rs_push(q[2, zs[zi], top, :], 0, 0, zi)
        rs_push(q[2, zs[zi], bottom, :], 1, 0, zi)

    def rs_direct(zi):
        rs_push(q[1, zs[zi], bottom, :], 0, 1, zi)
        rs_push(q[3, zs[zi], top, :], 1, 1, zi)

    def rs_second(zi):
        rs_push(q[1, zs[zi], top, :] + rs_wait(0, 0, zi), 0, 2, zi)
        rs_push(q[3, zs[zi], bottom, :] + rs_wait(1, 0, zi), 1, 2, zi)

    share(2)
    take(half(xl, z, c, 0), 3, 4)
    push_same(quarter(xl, z, c, 0, 0), ag_send, ag_recv, 12, right)
    take(half(xr, z, c, 0), 4, 5)
    push_same(quarter(xr, z, c, 0, 1), ag_send, ag_recv, 13, left)
    take(half(x, other, c, 1), 5, 6)
    rs_first(0)
    share(1)
    share(3)
    take(quarter(xo, z, c, 1, 0), 7, 7)
    push_same(quarter(xo, z, c, 1, 0), ag_send, ag_recv, 14, zdev)
    take(quarter(xo, z, c, 1, 1), 9, 8)
    push_same(quarter(xo, z, c, 1, 1), ag_send, ag_recv, 15, zdev)
    take(half(xl, other, c, 0), 10, 9)
    push_same(quarter(xl, other, c, 0, 0), ag_send, ag_recv, 16, right)
    take(half(xr, other, c, 0), 11, 10)
    push_same(quarter(xr, other, c, 0, 1), ag_send, ag_recv, 17, left)
    rs_direct(0)
    share(0)

    loads[13].wait()

    def unit(dx, x_, z_, zi):
        u = x_ * 2 + z_
        cols = pl.ds(pl.multiple_of(u * 256, 256), 256)
        both = jnp.concatenate([acts[2 * u].reshape(1024, 128), acts[2 * u + 1].reshape(1024, 128)], axis=1)
        gtmp[...] = jnp.dot(got[...], both, preferred_element_type=F32)

        for k in range(7):
            rows = pl.ds(k * TILE, TILE)
            kept = decay_rate * mom[rows, cols] + gtmp[rows, :]
            gtmp[rows, :] = kept
            scaled = kept * basis[k : k + 1, cols]
            high = scaled.astype(BF16)
            low = (scaled - high.astype(F32)).astype(BF16)
            ycat[rows, :] = jnp.concatenate([high, low], axis=1)

        ptmp[...] = jnp.dot(ycat[...], segments[...], preferred_element_type=F32)
        lines = lax.dot_general(chooser, ycat[...], (((1,), (1,)), ((), ())), preferred_element_type=F32)
        p_own[zi, dx // 2, pl.ds(dx % 2 * 4, 4), :] = lines[:4]
        for k in range(7):
            rows = pl.ds(k * TILE, TILE)
            mom[rows, cols] = gtmp[rows, :] - ptmp[rows, :] * basis[k : k + 1, cols]

    sb = lambda x_, z_: block(x_, z_, 1 - c)
    sh = lambda x_, z_, h: half(x_, z_, 1 - c, h)

    def from_sib(ref, k):
        arrived(ref, sib_send, sib_recv, k)

    xs = (x, xl, xr, xo)

    def p_zh(group):
        p_all[group, zh, y] = p_own[group // 2, group % 2]
        mine = p_all.at[group, zh, y]
        for k, dev in enumerate(zh_devs):
            push(mine, mine, ps_send.at[group, k], ps_recv.at[group, k], dev)

    def p_y(group):
        for k in range(3):
            slot = p_all.at[group, (zh + 3 - k) % 4, y]
            remote(slot, slot, ps_send.at[group, k], ps_recv.at[group, k], sib).wait_recv()
        mine = p_all.at[group, :, y]
        for k, dev in enumerate(y_devs):
            push(mine, mine, py_send.at[group, k], py_recv.at[group, k], dev)

    def finish(group):
        for k in range(3):
            slot = p_all.at[group, :, (y + 3 - k) % 4]
            remote(slot, slot, py_send.at[group, k], py_recv.at[group, k], sib).wait_recv()
        tiles = p_all[group].reshape(8, 2, 8, 448)
        even, odd = tiles[:, 0], tiles[:, 1]
        lines = jnp.concatenate(
            [
                jnp.concatenate([even[:, rows], odd[:, rows]], axis=1).reshape(TILE, 448)
                for rows in (slice(0, 4), slice(4, 8))
            ],
            axis=0,
        )
        turned = jnp.transpose(lines)
        high = turned.astype(BF16)
        low = (turned - high.astype(F32)).astype(BF16)
        for k in range(2):
            own_lanes = slice(k * TILE, (k + 1) * TILE)
            lhs[k] = jnp.concatenate([high[:, own_lanes], low[:, own_lanes], high[:, own_lanes]], axis=1)
            u = xs[group % 2 * 2 + k] * 2 + (z, other)[group // 2]
            cols = pl.ds(pl.multiple_of(u * 256, 256), 256)
            for j in range(7):
                rows = pl.ds(j * TILE, TILE)
                terms = right_side[u, j]
                full = jnp.concatenate([terms[:TILE], terms], axis=0)
                upd[rows, cols] = jnp.dot(lhs[k, rows, :], full, preferred_element_type=F32).astype(BF16)

    from_sib(sb(x, z), 0)
    unit(0, x, z, 0)
    take(quarter(xo, z, c, 0, 0), 12, 11)
    take(quarter(xo, z, c, 0, 1), 13, 12)
    take(half(xl, other, c, 1), 6, 13)
    take(half(xr, other, c, 1), 8, 14)
    from_sib(sh(xl, z, 1), 1)
    from_sib(sh(xl, z, 0), 4)
    unit(1, xl, z, 0)
    p_zh(0)
    from_sib(sh(xr, z, 1), 2)
    from_sib(sh(xr, z, 0), 5)
    unit(2, xr, z, 0)
    from_sib(quarter(xo, z, 1 - c, 1, 0), 7)
    from_sib(quarter(xo, z, 1 - c, 1, 1), 8)
    from_sib(quarter(xo, z, 1 - c, 0, 0), 11)
    from_sib(quarter(xo, z, 1 - c, 0, 1), 12)
    unit(3, xo, z, 0)
    p_zh(1)
    rs_second(0)
    rs_first(1)
    rs_direct(1)
    take(quarter(xo, other, c, 0, 0), 16, 15)
    take(quarter(xo, other, c, 0, 1), 17, 16)
    take(quarter(xo, other, c, 1, 0), 14, 17)
    take(quarter(xo, other, c, 1, 1), 15, 18)
    from_sib(sh(x, other, 0), 3)
    from_sib(sh(x, other, 1), 6)
    unit(0, x, other, 1)
    p_y(0)
    from_sib(sh(xl, other, 0), 9)
    from_sib(sh(xl, other, 1), 13)
    unit(1, xl, other, 1)
    p_zh(2)
    p_y(1)
    from_sib(sh(xr, other, 0), 10)
    from_sib(sh(xr, other, 1), 14)
    unit(2, xr, other, 1)
    from_sib(quarter(xo, other, 1 - c, 0, 0), 15)
    from_sib(quarter(xo, other, 1 - c, 0, 1), 16)
    from_sib(quarter(xo, other, 1 - c, 1, 0), 17)
    from_sib(quarter(xo, other, 1 - c, 1, 1), 18)
    unit(3, xo, other, 1)
    p_zh(3)
    p_y(2)
    def x_sum(zi):
        return (
            q[0, zs[zi], top, :] + rs_wait(0, 2, zi) + rs_wait(1, 1, zi),
            q[0, zs[zi], bottom, :] + rs_wait(0, 1, zi) + rs_wait(1, 2, zi),
        )

    for k, value in enumerate(x_sum(0)):
        encode(sz.at[k], value)
        push(sz.at[k], rz.at[k], zs_send.at[k], zs_recv.at[k], zdev)
    rs_second(1)

    p_y(3)
    finish(0)
    finish(1)
    finish(2)
    finish(3)

    sums = x_sum(1)
    for k in range(2):
        remote(sz.at[k], rz.at[k], zs_send.at[k], zs_recv.at[k], zdev).wait_recv()
        ig[pl.ds(k * 512, 512), :] = (sums[k] + decoded(rz.at[k])).astype(BF16)
    for copy in sent:
        copy.wait_send()


def store(*refs):
    sources, targets, sems = refs[:3], refs[3:6], refs[6]
    copies = []
    for k, (source, target) in enumerate(zip(sources, targets)):
        parts = 7 if source.shape[0] == 448 else 4
        height = source.shape[0] // parts
        for part in range(parts):
            rows = pl.ds(part * height, height)
            copies.append(pltpu.make_async_copy(source.at[rows], target.at[rows], sems.at[k, part]))
    for copy in copies:
        copy.start()
    for copy in copies:
        copy.wait()


def body(activations, grad_out, weight, momentum, freq_rows):
    hbm = pl.BlockSpec(memory_space=pltpu.HBM)
    vmem = pl.BlockSpec(memory_space=pltpu.VMEM)
    dma = pltpu.SemaphoreType.DMA
    outs = (
        jax.ShapeDtypeStruct((1024, 128), BF16),
        jax.ShapeDtypeStruct((448, 2048), F32),
        jax.ShapeDtypeStruct((448, 2048), BF16),
    )
    table, terms = cosine_tables()
    input_grad, momentum_out, update = pl.pallas_call(
        kernel,
        out_shape=outs,
        in_specs=[hbm] * 7,
        out_specs=(vmem, vmem, vmem),
        scratch_shapes=[
            pltpu.VMEM((16, 2, 2, 256, 128), BF16),
            pltpu.VMEM((448, 1024), BF16),
            pltpu.VMEM((2, 1024, 448), BF16),
            pltpu.VMEM((2, 8, 448, 128), BF16),
            pltpu.VMEM((4, 2, 1024, 128), F32),
            pltpu.VMEM((2, 3, 2, 528, 128), jnp.int16),
            pltpu.VMEM((2, 3, 2, 528, 128), jnp.int16),
            pltpu.VMEM((2, 528, 128), jnp.int16),
            pltpu.VMEM((2, 528, 128), jnp.int16),
            pltpu.VMEM((448, 256), F32),
            pltpu.VMEM((448, 256), F32),
            pltpu.VMEM((448, 512), BF16),
            pltpu.VMEM((7, 2048), F32),
            pltpu.VMEM((512, 256), BF16),
            pltpu.VMEM((8, 7, 128, 256), BF16),
            pltpu.VMEM((2, 448, 192), BF16),
            pltpu.VMEM((2, 2, 8, 448), F32),
            pltpu.VMEM((4, 4, 4, 8, 448), F32),
            pltpu.VMEM((7, 16, 32), jnp.int32),
            pltpu.VMEM((TILE, 128), F32),
            pltpu.VMEM((TILE, 512), BF16),
            dma((14,)),
            dma((9,)), dma((9,)),
            dma((18,)), dma((18,)),
            dma((19,)), dma((19,)),
            dma((12,)), dma((12,)),
            dma((2,)), dma((2,)),
            dma((4, 3)), dma((4, 3)),
            dma((4, 3)), dma((4, 3)),
        ],
        compiler_params=pltpu.CompilerParams(
            collective_id=0, has_side_effects=True, vmem_limit_bytes=40 * 1024 * 1024
        ),
        name="demo_step",
    )(
        *(
            pltpu.with_memory_space_constraint(value, pltpu.HBM)
            for value in (
                activations.reshape(2, 2, 256, 128),
                grad_out.T,
                weight.T,
                momentum[0].T,
                freq_rows.transpose(2, 0, 1),
                jnp.asarray(table),
                jnp.asarray(terms),
            )
        )
    )
    input_grad, momentum_out, update = pl.pallas_call(
        store,
        out_shape=outs,
        in_specs=[pl.BlockSpec(memory_space=pl.ANY)] * 3,
        out_specs=(hbm, hbm, hbm),
        scratch_shapes=[dma((3, 7))],
        compiler_params=pltpu.CompilerParams(vmem_limit_bytes=4 * 1024 * 1024),
        name="store_results",
    )(*(pltpu.with_memory_space_constraint(value, pltpu.VMEM) for value in (input_grad, momentum_out, update)))
    return input_grad, momentum_out.T[None], update.T


def solution(mesh):
    placed = (
        P("replica", "tensor"),
        P("replica", "tensor"),
        P(None, "tensor"),
        P("replica", None, "tensor"),
        P(None, None, "tensor"),
    )
    return jax.shard_map(
        body,
        mesh=mesh,
        in_specs=placed,
        out_specs=(P("replica", "tensor"), P("replica", None, "tensor"), P(None, "tensor")),
        check_vma=False,
    )
```

```python
import functools

import jax
import jax.numpy as jnp
import numpy as np
from jax import lax
from jax.experimental import pallas as pl
from jax.experimental.pallas import tpu as pltpu
from jax.sharding import PartitionSpec as P

MESH = pl.DeviceIdType.MESH
F32 = jnp.float32
BF16 = jnp.bfloat16

TILE = 64
decay_rate = 0.9


def cosine_tables():
    freq = np.arange(TILE, dtype=np.float64)[:, None]
    place = np.arange(TILE, dtype=np.float64)[None, :]
    values = np.cos(np.pi * (2.0 * place + 1.0) * freq / (2.0 * TILE)) * np.sqrt(2.0 / TILE)
    values = np.where(freq == 0.0, values / np.sqrt(2.0), values).astype(np.float32)
    high = values.astype(BF16)
    low = (values - high.astype(np.float32)).astype(BF16)
    return np.concatenate([values] * 2, axis=1), np.concatenate([high] * 4 + [low] * 4, axis=1)


def kernel(
    act_hbm, go_hbm, w_hbm, mom_hbm, freq_hbm, cos_hbm, terms_hbm,
    ig, mom, upd,
    acts, got, go, wt, q, sx, rx, sz, rz, gtmp, ptmp, ycat, basis, segments, right_side, lhs, p_own, p_all,
    freq_ref, cos_ref, terms_ref,
    load_sem, ex_send, ex_recv, ag_send, ag_recv, sib_send, sib_recv,
    rs_send, rs_recv, zs_send, zs_recv, ps_send, ps_recv, py_send, py_recv,
):
    r = lax.axis_index("replica")
    t = lax.axis_index("tensor")
    x, z, c = t // 4, (t // 2) % 2, t % 2
    zh, y = r // 4, r % 4
    other = 1 - z

    def at(x_, z_, c_):
        return (r, x_ * 4 + z_ * 2 + c_)

    xr, xl, xo = (x + 1) % 4, (x + 3) % 4, (x + 2) % 4
    right, left = at(xr, z, c), at(xl, z, c)
    zdev, sib = at(x, other, c), at(x, z, 1 - c)
    zh_devs = [(((zh + k) % 4) * 4 + y, t) for k in (1, 2, 3)]
    y_devs = [(zh * 4 + (y + k) % 4, t) for k in (1, 2, 3)]

    def w_cols(u, c_):
        return w_hbm.at[:, pl.ds(pl.multiple_of((2 * u + c_) * 128, 128), 128)]

    loads = [
        pltpu.make_async_copy(go_hbm, got, load_sem.at[0]),
        pltpu.make_async_copy(act_hbm, acts.at[t], load_sem.at[1]),
        pltpu.make_async_copy(freq_hbm, freq_ref, load_sem.at[2]),
        pltpu.make_async_copy(cos_hbm, cos_ref, load_sem.at[3]),
        pltpu.make_async_copy(terms_hbm, terms_ref, load_sem.at[4]),
    ] + [pltpu.make_async_copy(w_cols(u, c), wt.at[0, u], load_sem.at[5 + u]) for u in range(8)]
    loads.append(pltpu.make_async_copy(mom_hbm, mom, load_sem.at[13]))
    for load in loads:
        load.start()

    barrier = pltpu.get_barrier_semaphore()
    peers = [right, left, zdev, sib] + zh_devs + y_devs
    for peer in peers:
        pl.semaphore_signal(barrier, inc=1, device_id=peer, device_id_type=MESH)

    loads[0].wait()
    go[0] = jnp.transpose(got[...])
    loads[1].wait()
    pl.semaphore_wait(barrier, len(peers))

    def remote(src, dst, send, recv, dev):
        return pltpu.make_async_remote_copy(
            src_ref=src, dst_ref=dst, send_sem=send, recv_sem=recv, device_id=dev, device_id_type=MESH
        )

    sent = []

    def push(src, dst, send, recv, dev):
        copy = remote(src, dst, send, recv, dev)
        copy.start()
        sent.append(copy)

    def block(x_, z_, c_):
        return acts.at[x_ * 4 + z_ * 2 + c_]

    def half(x_, z_, c_, h):
        return acts.at[x_ * 4 + z_ * 2 + c_, h]

    def quarter(x_, z_, c_, h, k):
        return acts.at[x_ * 4 + z_ * 2 + c_, h, k]

    def push_same(ref, sends, recvs, k, dev):
        push(ref, ref, sends.at[k], recvs.at[k], dev)

    def arrived(ref, sends, recvs, k):
        remote(ref, ref, sends.at[k], recvs.at[k], sib).wait_recv()

    def own(h):
        return half(x, z, c, h)

    push_same(own(1), ag_send, ag_recv, 0, right)
    push_same(own(1), ag_send, ag_recv, 1, left)
    push_same(own(0), ag_send, ag_recv, 2, zdev)
    push_same(own(0), ag_send, ag_recv, 3, right)
    push_same(own(0), ag_send, ag_recv, 4, left)
    push_same(own(1), ag_send, ag_recv, 5, zdev)
    push(go.at[0], go.at[1], ex_send.at[0], ex_recv.at[0], sib)
    for u in range(8):
        push(w_cols(u, 1 - c), wt.at[1, u], ex_send.at[1 + u], ex_recv.at[1 + u], sib)
    push_same(block(x, z, c), sib_send, sib_recv, 0, sib)

    for load in loads[2:5]:
        load.wait()

    mine = jnp.concatenate([freq_ref[k, pl.ds(r, 1), :] for k in range(7)], axis=0)
    first = lax.broadcasted_iota(jnp.int32, (7, 128), 1) < TILE
    spread = jnp.concatenate(
        [jnp.where(first, mine[:, 2 * k : 2 * k + 1], mine[:, 2 * k + 1 : 2 * k + 2]) for k in range(16)], axis=1
    )

    def pick(k, so_far):
        row = jnp.concatenate([cos_ref[pl.ds(k, 1), :]] * 16, axis=1)
        return jnp.where(spread == k, row, so_far)

    basis[...] = lax.fori_loop(0, TILE, pick, jnp.zeros((7, 2048), F32))

    segments[...] = (
        lax.broadcasted_iota(jnp.int32, (512, 256), 0) % 256 // TILE
        == lax.broadcasted_iota(jnp.int32, (512, 256), 1) // TILE
    ).astype(F32).astype(BF16)
    chooser = (
        lax.broadcasted_iota(jnp.int32, (8, 512), 1) % 256 // TILE
        == lax.broadcasted_iota(jnp.int32, (8, 512), 0)
    ).astype(F32).astype(BF16)

    widen = (
        lax.broadcasted_iota(jnp.int32, (TILE, 16), 0) // 4 == lax.broadcasted_iota(jnp.int32, (TILE, 16), 1)
    ).astype(F32).astype(BF16)
    wide = jnp.concatenate(
        [jnp.dot(widen, freq_ref[k].astype(F32).astype(BF16), preferred_element_type=F32) for k in range(7)], axis=0
    )
    keep = (
        lax.broadcasted_iota(jnp.int32, (448, 32), 0) % 4 == lax.broadcasted_iota(jnp.int32, (448, 32), 1) % 4
    )
    narrow = (
        lax.broadcasted_iota(jnp.int32, (32, 8), 0) // 4 == lax.broadcasted_iota(jnp.int32, (32, 8), 1)
    ).astype(F32).astype(BF16)
    columns = jnp.dot(jnp.where(keep, wide, 0.0).astype(BF16), narrow, preferred_element_type=F32)
    freq_lane = lax.broadcasted_iota(jnp.int32, (448, TILE), 1).astype(F32)
    same = (
        lax.broadcasted_iota(jnp.int32, (TILE, 256), 0) % 4 == lax.broadcasted_iota(jnp.int32, (TILE, 256), 1) // TILE
    )
    for u in range(8):
        hot = (columns[:, u : u + 1] == freq_lane).astype(F32).astype(BF16)
        both = jnp.dot(hot, terms_ref[...], preferred_element_type=F32)
        for k in range(7):
            rows = both[k * TILE : (k + 1) * TILE]
            right_side[u, k, pl.ds(0, TILE), :] = jnp.where(same, rows[:, :256], 0.0).astype(BF16)
            right_side[u, k, pl.ds(TILE, TILE), :] = jnp.where(same, rows[:, 256:], 0.0).astype(BF16)

    def take(ref, k, sib_k):
        arrived(ref, ag_send, ag_recv, k)
        push_same(ref, sib_send, sib_recv, sib_k, sib)

    take(half(xl, z, c, 1), 0, 1)
    push_same(half(xl, z, c, 1), ag_send, ag_recv, 6, zdev)
    push_same(quarter(xl, z, c, 1, 0), ag_send, ag_recv, 7, right)
    take(half(xr, z, c, 1), 1, 2)
    push_same(half(xr, z, c, 1), ag_send, ag_recv, 8, zdev)
    push_same(quarter(xr, z, c, 1, 1), ag_send, ag_recv, 9, left)
    take(half(x, other, c, 0), 2, 3)
    push_same(half(x, other, c, 0), ag_send, ag_recv, 10, right)
    push_same(half(x, other, c, 0), ag_send, ag_recv, 11, left)

    for load in loads[5:13]:
        load.wait()
    remote(go.at[0], go.at[1], ex_send.at[0], ex_recv.at[0], sib).wait_recv()
    for u in range(8):
        remote(wt.at[0, u], wt.at[1, u], ex_send.at[1 + u], ex_recv.at[1 + u], sib).wait_recv()

    def share(dx):
        dest = (x + dx) % 4

        @pl.loop(0, 4)
        def _(k):
            rows = pl.ds(pl.multiple_of(k * 256, 256), 256)
            total = jnp.zeros((256, 256), F32)
            for part in range(2):
                pair = jnp.concatenate([wt[part, dest * 2], wt[part, dest * 2 + 1]], axis=1)
                total += jnp.dot(go[part, rows, :], pair, preferred_element_type=F32)
            q[dx, 0, rows, :] = total[:, :128]
            q[dx, 1, rows, :] = total[:, 128:]

    top, bottom = pl.ds(0, 512), pl.ds(512, 512)
    zs = (other, z)

    def encode(slot, value):
        exponents = []
        for k in range(8):
            part = value[k * TILE : (k + 1) * TILE]
            largest = jnp.max(jnp.abs(part), axis=0, keepdims=True)
            exponent = jnp.floor(jnp.log2(jnp.maximum(largest, 1e-30))) + 1.0
            whole = jnp.floor(part * (32000.0 * jnp.exp2(-exponent)) + 0.5)
            slot[pl.ds(k * TILE, TILE), :] = whole.astype(jnp.int32).astype(jnp.int16)
            exponents.append(exponent)
        tail = jnp.concatenate(exponents + [jnp.zeros((8, 128), F32)], axis=0)
        slot[pl.ds(512, 16), :] = tail.astype(jnp.int32).astype(jnp.int16)

    def decoded(slot):
        scale = jnp.exp2(slot[pl.ds(512, 16), :].astype(jnp.int32).astype(F32)) * (1.0 / 32000.0)
        return jnp.concatenate(
            [
                slot[pl.ds(k * TILE, TILE), :].astype(jnp.int32).astype(F32) * scale[k : k + 1]
                for k in range(8)
            ],
            axis=0,
        )

    def rs_push(value, direction, kind, zi):
        k = (direction * 3 + kind) * 2 + zi
        src = sx.at[direction, kind, zi]
        encode(src, value)
        push(src, rx.at[direction, kind, zi], rs_send.at[k], rs_recv.at[k], (right, left)[direction])

    def rs_wait(direction, kind, zi):
        k = (direction * 3 + kind) * 2 + zi
        slot = rx.at[direction, kind, zi]
        remote(slot, slot, rs_send.at[k], rs_recv.at[k], sib).wait_recv()
        return decoded(slot)

    def rs_first(zi):
        rs_push(q[2, zs[zi], top, :], 0, 0, zi)
        rs_push(q[2, zs[zi], bottom, :], 1, 0, zi)

    def rs_direct(zi):
        rs_push(q[1, zs[zi], bottom, :], 0, 1, zi)
        rs_push(q[3, zs[zi], top, :], 1, 1, zi)

    def rs_second(zi):
        rs_push(q[1, zs[zi], top, :] + rs_wait(0, 0, zi), 0, 2, zi)
        rs_push(q[3, zs[zi], bottom, :] + rs_wait(1, 0, zi), 1, 2, zi)

    share(2)
    take(half(xl, z, c, 0), 3, 4)
    push_same(quarter(xl, z, c, 0, 0), ag_send, ag_recv, 12, right)
    take(half(xr, z, c, 0), 4, 5)
    push_same(quarter(xr, z, c, 0, 1), ag_send, ag_recv, 13, left)
    take(half(x, other, c, 1), 5, 6)
    rs_first(0)
    share(1)
    share(3)
    take(quarter(xo, z, c, 1, 0), 7, 7)
    push_same(quarter(xo, z, c, 1, 0), ag_send, ag_recv, 14, zdev)
    take(quarter(xo, z, c, 1, 1), 9, 8)
    push_same(quarter(xo, z, c, 1, 1), ag_send, ag_recv, 15, zdev)
    take(half(xl, other, c, 0), 10, 9)
    push_same(quarter(xl, other, c, 0, 0), ag_send, ag_recv, 16, right)
    take(half(xr, other, c, 0), 11, 10)
    push_same(quarter(xr, other, c, 0, 1), ag_send, ag_recv, 17, left)
    rs_direct(0)
    share(0)

    loads[13].wait()

    def unit(dx, x_, z_, zi):
        u = x_ * 2 + z_
        cols = pl.ds(pl.multiple_of(u * 256, 256), 256)
        both = jnp.concatenate([acts[2 * u].reshape(1024, 128), acts[2 * u + 1].reshape(1024, 128)], axis=1)
        gtmp[dx] = jnp.dot(got[...], both, preferred_element_type=F32)

        for k in range(7):
            rows = pl.ds(k * TILE, TILE)
            kept = decay_rate * mom[rows, cols] + gtmp[dx, rows, :]
            gtmp[dx, rows, :] = kept
            scaled = kept * basis[k : k + 1, cols]
            high = scaled.astype(BF16)
            low = (scaled - high.astype(F32)).astype(BF16)
            ycat[dx, rows, :] = jnp.concatenate([high, low], axis=1)

        lines = lax.dot_general(chooser, ycat[dx], (((1,), (1,)), ((), ())), preferred_element_type=F32)
        p_own[zi, dx // 2, pl.ds(dx % 2 * 4, 4), :] = lines[:4]
        if zi == 0:
            settle(dx, x_, z_)

    def settle(dx, x_, z_):
        cols = pl.ds(pl.multiple_of((x_ * 2 + z_) * 256, 256), 256)
        ptmp[...] = jnp.dot(ycat[dx], segments[...], preferred_element_type=F32)
        for k in range(7):
            rows = pl.ds(k * TILE, TILE)
            mom[rows, cols] = gtmp[dx, rows, :] - ptmp[rows, :] * basis[k : k + 1, cols]

    sb = lambda x_, z_: block(x_, z_, 1 - c)
    sh = lambda x_, z_, h: half(x_, z_, 1 - c, h)

    def from_sib(ref, k):
        arrived(ref, sib_send, sib_recv, k)

    xs = (x, xl, xr, xo)

    def p_zh(group):
        p_all[group, zh, y] = p_own[group // 2, group % 2]
        mine = p_all.at[group, zh, y]
        for k, dev in enumerate(zh_devs):
            push(mine, mine, ps_send.at[group, k], ps_recv.at[group, k], dev)

    def p_y(group):
        for k in range(3):
            slot = p_all.at[group, (zh + 3 - k) % 4, y]
            remote(slot, slot, ps_send.at[group, k], ps_recv.at[group, k], sib).wait_recv()
        mine = p_all.at[group, :, y]
        for k, dev in enumerate(y_devs):
            push(mine, mine, py_send.at[group, k], py_recv.at[group, k], dev)

    def finish(group):
        for k in range(3):
            slot = p_all.at[group, :, (y + 3 - k) % 4]
            remote(slot, slot, py_send.at[group, k], py_recv.at[group, k], sib).wait_recv()
        tiles = p_all[group].reshape(8, 2, 8, 448)
        even, odd = tiles[:, 0], tiles[:, 1]
        lines = jnp.concatenate(
            [
                jnp.concatenate([even[:, rows], odd[:, rows]], axis=1).reshape(TILE, 448)
                for rows in (slice(0, 4), slice(4, 8))
            ],
            axis=0,
        )
        turned = jnp.transpose(lines)
        high = turned.astype(BF16)
        low = (turned - high.astype(F32)).astype(BF16)
        for k in range(2):
            own_lanes = slice(k * TILE, (k + 1) * TILE)
            lhs[k] = jnp.concatenate([high[:, own_lanes], low[:, own_lanes], high[:, own_lanes]], axis=1)
            u = xs[group % 2 * 2 + k] * 2 + (z, other)[group // 2]
            cols = pl.ds(pl.multiple_of(u * 256, 256), 256)
            for j in range(7):
                rows = pl.ds(j * TILE, TILE)
                terms = right_side[u, j]
                full = jnp.concatenate([terms[:TILE], terms], axis=0)
                upd[rows, cols] = jnp.dot(lhs[k, rows, :], full, preferred_element_type=F32).astype(BF16)

    from_sib(sb(x, z), 0)
    unit(0, x, z, 0)
    take(quarter(xo, z, c, 0, 0), 12, 11)
    take(quarter(xo, z, c, 0, 1), 13, 12)
    take(half(xl, other, c, 1), 6, 13)
    take(half(xr, other, c, 1), 8, 14)
    from_sib(sh(xl, z, 1), 1)
    from_sib(sh(xl, z, 0), 4)
    unit(1, xl, z, 0)
    p_zh(0)
    from_sib(sh(xr, z, 1), 2)
    from_sib(sh(xr, z, 0), 5)
    unit(2, xr, z, 0)
    from_sib(quarter(xo, z, 1 - c, 1, 0), 7)
    from_sib(quarter(xo, z, 1 - c, 1, 1), 8)
    from_sib(quarter(xo, z, 1 - c, 0, 0), 11)
    from_sib(quarter(xo, z, 1 - c, 0, 1), 12)
    unit(3, xo, z, 0)
    p_zh(1)
    rs_second(0)
    rs_first(1)
    rs_direct(1)
    take(quarter(xo, other, c, 0, 0), 16, 15)
    take(quarter(xo, other, c, 0, 1), 17, 16)
    take(quarter(xo, other, c, 1, 0), 14, 17)
    take(quarter(xo, other, c, 1, 1), 15, 18)
    from_sib(sh(x, other, 0), 3)
    from_sib(sh(x, other, 1), 6)
    unit(0, x, other, 1)
    p_y(0)
    from_sib(sh(xl, other, 0), 9)
    from_sib(sh(xl, other, 1), 13)
    unit(1, xl, other, 1)
    p_zh(2)
    p_y(1)
    from_sib(sh(xr, other, 0), 10)
    from_sib(sh(xr, other, 1), 14)
    unit(2, xr, other, 1)
    from_sib(quarter(xo, other, 1 - c, 0, 0), 15)
    from_sib(quarter(xo, other, 1 - c, 0, 1), 16)
    from_sib(quarter(xo, other, 1 - c, 1, 0), 17)
    from_sib(quarter(xo, other, 1 - c, 1, 1), 18)
    unit(3, xo, other, 1)
    p_zh(3)
    p_y(2)
    def x_sum(zi):
        return (
            q[0, zs[zi], top, :] + rs_wait(0, 2, zi) + rs_wait(1, 1, zi),
            q[0, zs[zi], bottom, :] + rs_wait(0, 1, zi) + rs_wait(1, 2, zi),
        )

    for k, value in enumerate(x_sum(0)):
        encode(sz.at[k], value)
        push(sz.at[k], rz.at[k], zs_send.at[k], zs_recv.at[k], zdev)
    rs_second(1)

    settle(0, x, other)
    settle(1, xl, other)
    p_y(3)
    settle(2, xr, other)
    settle(3, xo, other)
    finish(0)
    finish(1)
    finish(2)
    finish(3)

    sums = x_sum(1)
    for k in range(2):
        remote(sz.at[k], rz.at[k], zs_send.at[k], zs_recv.at[k], zdev).wait_recv()
        ig[pl.ds(k * 512, 512), :] = (sums[k] + decoded(rz.at[k])).astype(BF16)
    for copy in sent:
        copy.wait_send()


def store(*refs):
    sources, targets, sems = refs[:3], refs[3:6], refs[6]
    copies = []
    for k, (source, target) in enumerate(zip(sources, targets)):
        parts = 7 if source.shape[0] == 448 else 4
        height = source.shape[0] // parts
        for part in range(parts):
            rows = pl.ds(part * height, height)
            copies.append(pltpu.make_async_copy(source.at[rows], target.at[rows], sems.at[k, part]))
    for copy in copies:
        copy.start()
    for copy in copies:
        copy.wait()


def body(activations, grad_out, weight, momentum, freq_rows):
    hbm = pl.BlockSpec(memory_space=pltpu.HBM)
    vmem = pl.BlockSpec(memory_space=pltpu.VMEM)
    dma = pltpu.SemaphoreType.DMA
    outs = (
        jax.ShapeDtypeStruct((1024, 128), BF16),
        jax.ShapeDtypeStruct((448, 2048), F32),
        jax.ShapeDtypeStruct((448, 2048), BF16),
    )
    table, terms = cosine_tables()
    input_grad, momentum_out, update = pl.pallas_call(
        kernel,
        out_shape=outs,
        in_specs=[hbm] * 7,
        out_specs=(vmem, vmem, vmem),
        scratch_shapes=[
            pltpu.VMEM((16, 2, 2, 256, 128), BF16),
            pltpu.VMEM((448, 1024), BF16),
            pltpu.VMEM((2, 1024, 448), BF16),
            pltpu.VMEM((2, 8, 448, 128), BF16),
            pltpu.VMEM((4, 2, 1024, 128), F32),
            pltpu.VMEM((2, 3, 2, 528, 128), jnp.int16),
            pltpu.VMEM((2, 3, 2, 528, 128), jnp.int16),
            pltpu.VMEM((2, 528, 128), jnp.int16),
            pltpu.VMEM((2, 528, 128), jnp.int16),
            pltpu.VMEM((4, 448, 256), F32),
            pltpu.VMEM((448, 256), F32),
            pltpu.VMEM((4, 448, 512), BF16),
            pltpu.VMEM((7, 2048), F32),
            pltpu.VMEM((512, 256), BF16),
            pltpu.VMEM((8, 7, 128, 256), BF16),
            pltpu.VMEM((2, 448, 192), BF16),
            pltpu.VMEM((2, 2, 8, 448), F32),
            pltpu.VMEM((4, 4, 4, 8, 448), F32),
            pltpu.VMEM((7, 16, 32), jnp.int32),
            pltpu.VMEM((TILE, 128), F32),
            pltpu.VMEM((TILE, 512), BF16),
            dma((14,)),
            dma((9,)), dma((9,)),
            dma((18,)), dma((18,)),
            dma((19,)), dma((19,)),
            dma((12,)), dma((12,)),
            dma((2,)), dma((2,)),
            dma((4, 3)), dma((4, 3)),
            dma((4, 3)), dma((4, 3)),
        ],
        compiler_params=pltpu.CompilerParams(
            collective_id=0, has_side_effects=True, vmem_limit_bytes=40 * 1024 * 1024
        ),
        name="demo_step",
    )(
        *(
            pltpu.with_memory_space_constraint(value, pltpu.HBM)
            for value in (
                activations.reshape(2, 2, 256, 128),
                grad_out.T,
                weight.T,
                momentum[0].T,
                freq_rows.transpose(2, 0, 1),
                jnp.asarray(table),
                jnp.asarray(terms),
            )
        )
    )
    input_grad, momentum_out, update = pl.pallas_call(
        store,
        out_shape=outs,
        in_specs=[pl.BlockSpec(memory_space=pl.ANY)] * 3,
        out_specs=(hbm, hbm, hbm),
        scratch_shapes=[dma((3, 7))],
        compiler_params=pltpu.CompilerParams(vmem_limit_bytes=4 * 1024 * 1024),
        name="store_results",
    )(*(pltpu.with_memory_space_constraint(value, pltpu.VMEM) for value in (input_grad, momentum_out, update)))
    return input_grad, momentum_out.T[None], update.T


def solution(mesh):
    placed = (
        P("replica", "tensor"),
        P("replica", "tensor"),
        P(None, "tensor"),
        P("replica", None, "tensor"),
        P(None, None, "tensor"),
    )
    return jax.shard_map(
        body,
        mesh=mesh,
        in_specs=placed,
        out_specs=(P("replica", "tensor"), P("replica", None, "tensor"), P(None, "tensor")),
        check_vma=False,
    )
```
